256 devices in a mesh: comp: 2 (over y_hi), tile: 128 (over y_lo, x, z, core).
Axes of the slice: x: 4, y: 4 (y_hi: 2, y_lo: 2; y = y_hi * 2 + y_lo), z: 8, core: 2. Of those that a mesh axis runs over, the one named last changes fastest.
Arguments:
- air_winds_heights: float32 [3, 16, 2048, 2048], P(None, None, 'tile', 'comp'), may hold values from -6 to 6
- exchange_coefficient_air: float32 [2048, 2048], P('tile', 'comp'), may hold values from 0.5 to 2
- air_seen_warmness: float32 [2048, 2048], P('tile', 'comp'), may hold values from 1 to 3
- marine_flow_vectors: float32 [2, 10, 1024, 1024], P(None, None, 'tile', 'comp'), may hold values from -6 to 6
- marine_warmness: float32 [1024, 1024], P('tile', 'comp'), may hold values from -6 to 6
- water_indicator: int32 [1024, 1024], P('tile', 'comp'), may hold values 0 or 1
- partner_air_tiles: int32 [8192, 4], P(('comp', 'tile')), may hold values from 0 to 16383, as said below
- partner_tally_each_tile: int32 [8192], P(('comp', 'tile')), may hold values from 2 to 4, as said below
- partner_overlay_shares: bfloat16 [8192, 4, 128, 128], P(('comp', 'tile')), may hold values from 0.0009994507 to 1
Outputs:
- atmosphere_next: float32 [3, 16, 2048, 2048], P(None, None, 'tile', 'comp')
- advanced_flows: float32 [2, 10, 1024, 1024], P(None, None, 'tile', 'comp')
- advanced_warmness: float32 [1024, 1024], P('tile', 'comp')
The draws below stay inside these ranges and needn't reach their ends.
Inputs may be any that keep to these rules, and one draw needn't show every extreme that they name: `partner_air_tiles`: every entry names an atmosphere block of the ocean block's own longitude half; for ocean block g with t = (g // 32) % 128 it lies from t * 128 - 8 to (t + 1) * 128 + 7, cut to the grid's blocks, and both ends of that range are named for every tile. `partner_tally_each_tile`: the first ocean block of every tile has all 4 slots live.
All inputs are finite; a program needn't handle non-finite values. No bound on the sum of `water_indicator` on one device may be relied on, other than what follows from the above.
Results may differ from the reference program's by a relative error of at most 0.0003.
Values sent between devices are 32-bit elements; how exact they have to be, the bound alone decides.
No kernel may reach another device: no remote copies, remote signals or barrier semaphores. Data moves between devices by JAX's collectives and lax.ppermute only.
A program may use at most 128 MiB of HBM per device.

```python
import math
import jax
import jax.numpy as jnp
from jax import lax

LEV_A = 16
MARINE_DEPTHS = 10
ALAT = 16
ALON = 1024
BLOCK = 128
NOV = 4
HB = 8
OLAT = 8
OLON = 512
NAB = 128
NOB = 32
TILES = 128
AIR_GRID_HEIGHT = 2048
AIR_GRID_WIDTH = 2048
MARINE_HEIGHT = 1024
MARINE_WIDTH = 1024
NOB_ALL = 8192
N_COMP = 2
N_TILE = 128


def draw_partner_air_tiles(key, part):
    block_ids = jnp.arange(NOB_ALL, dtype=jnp.int32)
    tile_ids = block_ids // NOB % TILES
    local_ids = block_ids % NOB
    low_end = tile_ids * NAB - HB
    span_width = NAB + 2 * HB
    offsets = jax.random.randint(key, (NOB_ALL, NOV), 0, span_width, dtype=jnp.int32)
    picked = low_end[:, None] + offsets
    first_slot = jnp.where(local_ids == 0, low_end, picked[:, 0])
    second_slot = jnp.where(local_ids == NOB - 1, low_end + span_width - 1, picked[:, 1])
    picked = jnp.concatenate([first_slot[:, None], second_slot[:, None], picked[:, 2:]], axis=1)
    return jnp.clip(picked, 0, NAB * TILES - 1).astype(jnp.int32)


def draw_partner_tally_each_tile(key, part):
    block_ids = jnp.arange(NOB_ALL, dtype=jnp.int32)
    drawn = jax.random.randint(key, (NOB_ALL,), 2, NOV + 1, dtype=jnp.int32)
    return jnp.where(block_ids % NOB == 0, NOV, drawn).astype(jnp.int32)


def place_ends(values, key, low, largest):
    extent = values.shape
    place = [jax.random.randint(jax.random.fold_in(key, axis), (), 0, extent[axis]) for axis in range(len(extent))]
    values = values.at[tuple(place)].set(low)
    longest = extent.index(max(extent))
    place[longest] = (place[longest] + 1) % extent[longest]
    return values.at[tuple(place)].set(largest)


def shard_levels(own_key, dims, pieces, low, top_value):
    def one(dim, parts):
        steps = jax.random.uniform(jax.random.fold_in(jax.random.fold_in(own_key, 6), dim), (parts,), jnp.float32, low / len(pieces), top_value / len(pieces))
        return jnp.repeat(jnp.exp(steps), dims[dim] // parts).reshape((-1,) + (1,) * (len(dims) - dim - 1))

    factor_of = one(*pieces[0])
    for cut in pieces[1:]:
        factor_of = factor_of * one(*cut)
    return factor_of


def normal_values(own_key, extent, deviation, most, pieces=(), kind=jnp.bfloat16):
    values = jax.random.normal(own_key, extent, jnp.float32) * deviation
    if len(pieces) > 0:
        values = shard_levels(own_key, extent, pieces, -0.22, 0.18) * values
    return jnp.clip(values, min=-most, max=most).astype(kind)


def setup_inputs(seed: int = 0) -> dict:
    arg_keys = jax.random.split(jax.random.key(seed), 10)
    return {
        "air_winds_heights": normal_values(arg_keys[0], (3, LEV_A, AIR_GRID_HEIGHT, AIR_GRID_WIDTH), 1.0, 6.0, ((2, 128), (3, 2)), jnp.float32),
        "exchange_coefficient_air": jnp.clip(jnp.exp(math.log(2.0) - 1.3862944 * jax.random.uniform(arg_keys[1], (AIR_GRID_HEIGHT, AIR_GRID_WIDTH), jnp.float32) ** shard_levels(arg_keys[1], (AIR_GRID_HEIGHT, AIR_GRID_WIDTH), ((0, 128), (1, 2)), -0.2, 0.2)), 0.5, 2.0),
        "air_seen_warmness": jnp.clip(1.0 + 2.0 * jax.random.uniform(arg_keys[2], (AIR_GRID_HEIGHT, AIR_GRID_WIDTH), jnp.float32) ** shard_levels(arg_keys[2], (AIR_GRID_HEIGHT, AIR_GRID_WIDTH), ((0, 128), (1, 2)), -0.2, 0.2), 1.0, 3.0),
        "marine_flow_vectors": normal_values(arg_keys[3], (2, MARINE_DEPTHS, MARINE_HEIGHT, MARINE_WIDTH), 1.0, 6.0, ((2, 128), (3, 2)), jnp.float32),
        "marine_warmness": normal_values(arg_keys[4], (MARINE_HEIGHT, MARINE_WIDTH), 1.0, 6.0, ((0, 128), (1, 2)), jnp.float32),
        "water_indicator": place_ends((jax.random.randint(arg_keys[5], (MARINE_HEIGHT, MARINE_WIDTH), 0, 10) < 7).astype(jnp.int32), jax.random.fold_in(arg_keys[5], 1), 0, 1),
        "partner_air_tiles": draw_partner_air_tiles(jax.random.fold_in(arg_keys[9], 71), 0),
        "partner_tally_each_tile": draw_partner_tally_each_tile(jax.random.fold_in(arg_keys[9], 71), 0),
        "partner_overlay_shares": jnp.clip(jnp.exp(math.log(1.0) - 6.9083047 * jax.random.uniform(arg_keys[8], (NOB_ALL, NOV, BLOCK, BLOCK), jnp.float32) ** shard_levels(arg_keys[8], (NOB_ALL, NOV, BLOCK, BLOCK), ((0, 256),), -0.2, 0.2)), 0.0009994507, 1.0).astype(jnp.bfloat16),
    }


step_atmos = 0.2
coriolis_atmos = 0.3
visc_atmos = 1.0
mixing_atmos = 0.5
gust_square = 0.25
step_ocean = 0.2
coriolis_ocean = 0.3
visc_ocean = 1.0
mixing_ocean = 0.5
heat_gain = 1.0
diffuse_ocean = 0.5

def vertical(joined_quantities):
    upper = jnp.concatenate([joined_quantities[1:], joined_quantities[-1:]], axis=0)
    lower = jnp.concatenate([joined_quantities[:1], joined_quantities[:-1]], axis=0)
    return upper - 2.0 * joined_quantities + lower

def stencil(bordered_argument):
    centre = bordered_argument[..., 1:-1, 1:-1]
    below_row = bordered_argument[..., :-2, 1:-1]
    above_row = bordered_argument[..., 2:, 1:-1]
    left_col = bordered_argument[..., 1:-1, :-2]
    right_col = bordered_argument[..., 1:-1, 2:]
    laplace = above_row + below_row + left_col + right_col - 4.0 * centre
    east_grad = 0.5 * (right_col - left_col)
    north_grad = 0.5 * (above_row - below_row)
    return (centre, laplace, east_grad, north_grad)

def advance(bordered_argument):
    centre, laplace, east_grad, north_grad = stencil(bordered_argument)
    zonal_flow, meridional_flow, depth_anomaly_sheet = (centre[0], centre[1], centre[2])
    new_east = zonal_flow + step_atmos * (coriolis_atmos * meridional_flow - east_grad[2] + visc_atmos * laplace[0] + mixing_atmos * vertical(zonal_flow))
    new_north = meridional_flow + step_atmos * (-coriolis_atmos * zonal_flow - north_grad[2] + visc_atmos * laplace[1] + mixing_atmos * vertical(meridional_flow))
    new_thick = depth_anomaly_sheet + step_atmos * (-(east_grad[0] + north_grad[1]) + visc_atmos * laplace[2] + mixing_atmos * vertical(depth_anomaly_sheet))
    return jnp.stack([new_east, new_north, new_thick])

def uppermost_sheet(joined_quantities, exchange_coefficient_air, air_seen_warmness):
    zonal_flow = joined_quantities[0, 0]
    meridional_flow = joined_quantities[1, 0]
    depth_anomaly_sheet = joined_quantities[2, 0]
    wind_speed = jnp.sqrt(zonal_flow * zonal_flow + meridional_flow * meridional_flow + gust_square)
    multiplier_coefficient = exchange_coefficient_air * wind_speed
    return jnp.stack([multiplier_coefficient * zonal_flow, multiplier_coefficient * meridional_flow, multiplier_coefficient * (air_seen_warmness - depth_anomaly_sheet)])

def remap_blocks(chosen, counts, weights):
    live_slots = (jnp.arange(weights.shape[1])[None, :] < counts[:, None]).astype(jnp.float32)
    masked = weights.astype(jnp.float32) * live_slots[:, :, None, None]
    numerator = jnp.einsum('fjsa,jsao->fjo', chosen, masked, precision=lax.Precision.HIGHEST)
    denominator = lax.optimization_barrier(jnp.sum(masked, axis=(1, 2)))
    return numerator / denominator[None]

def marine_drift_advance(bordered_argument, regridded_exchanges, sea_mask):
    centre, laplace, east_grad, north_grad = stencil(bordered_argument)
    levels = (centre.shape[0] - 1) // 2
    zonal_flow = centre[:levels]
    meridional_flow = centre[levels:2 * levels]
    warmth = centre[2 * levels]
    blank_levels = jnp.zeros_like(zonal_flow[1:])
    push_east = jnp.concatenate([regridded_exchanges[0][None], blank_levels], axis=0)
    push_north = jnp.concatenate([regridded_exchanges[1][None], blank_levels], axis=0)
    new_east = sea_mask * (zonal_flow + step_ocean * (coriolis_ocean * meridional_flow + visc_ocean * laplace[:levels] + mixing_ocean * vertical(zonal_flow) + push_east))
    new_north = sea_mask * (meridional_flow + step_ocean * (-coriolis_ocean * zonal_flow + visc_ocean * laplace[levels:2 * levels] + mixing_ocean * vertical(meridional_flow) + push_north))
    carried = zonal_flow[0] * east_grad[2 * levels] + meridional_flow[0] * north_grad[2 * levels]
    new_warm = warmth + sea_mask * step_ocean * (heat_gain * regridded_exchanges[2] - carried + diffuse_ocean * laplace[2 * levels])
    return (jnp.stack([new_east, new_north]), new_warm)

def reference(air_winds_heights, exchange_coefficient_air, air_seen_warmness, marine_flow_vectors, marine_warmness, water_indicator, partner_air_tiles, partner_tally_each_tile, partner_overlay_shares):
    joined_quantities = air_winds_heights
    for repeat in range(2):
        joined_quantities = advance(jnp.pad(joined_quantities, ((0, 0), (0, 0), (1, 1), (1, 1))))
    interface_exchanges = uppermost_sheet(joined_quantities, exchange_coefficient_air, air_seen_warmness)
    halves = interface_exchanges.reshape(3, N_TILE, ALAT, N_COMP, ALON).transpose(3, 0, 1, 2, 4).reshape(N_COMP, 3, N_TILE * NAB, BLOCK)
    groups = N_COMP * N_TILE
    sources = partner_air_tiles.reshape(groups, NOB, NOV)
    counts = partner_tally_each_tile.reshape(groups, NOB)
    weights = partner_overlay_shares.reshape(groups, NOB, NOV, BLOCK, BLOCK)
    half_ids = jnp.arange(groups, dtype=jnp.int32) // N_TILE

    def remap_tile(tile_items):
        source_rows, count_rows, weight_rows, half_id = tile_items
        chosen = jnp.take(halves[half_id], source_rows, axis=1)
        return remap_blocks(chosen, count_rows, weight_rows)
    regridded_exchanges = lax.map(remap_tile, (sources, counts, weights, half_ids))
    regridded_exchanges = regridded_exchanges.reshape(N_COMP, N_TILE, 3, OLAT, OLON).transpose(2, 1, 3, 0, 4).reshape(3, MARINE_HEIGHT, MARINE_WIDTH)
    joined_arrays = jnp.concatenate([marine_flow_vectors.reshape(2 * MARINE_DEPTHS, MARINE_HEIGHT, MARINE_WIDTH), marine_warmness[None]], axis=0)
    bordered_argument = jnp.pad(joined_arrays, ((0, 0), (1, 1), (1, 1)))
    advanced_flows, advanced_warmness = marine_drift_advance(bordered_argument, regridded_exchanges, water_indicator.astype(jnp.float32))
    return (joined_quantities, advanced_flows, advanced_warmness)
```

```python
import jax
import jax.numpy as jnp
from jax import lax
from jax.experimental import pallas as pl
from jax.experimental.pallas import tpu as pltpu
from jax.sharding import PartitionSpec as P

F32 = jnp.float32
LEV, ROWS, COLS = 16, 16, 1024
OLEV, OROWS, OCOLS = 10, 8, 512
WIDE = COLS + 128
OWIDE = OCOLS + 128
ANY = pl.BlockSpec(memory_space=pl.ANY)
SMEM = pl.BlockSpec(memory_space=pltpu.SMEM)


def lanes():
    return lax.broadcasted_iota(jnp.int32, (8, 128), 1)


def sublanes():
    return lax.broadcasted_iota(jnp.int32, (8, 128), 0)


def pack_kernel(x, ex, air, flow, warm, pay_a, pay_b, swp, dg_a, dg_b, xt, ft, wt, packed, sems):
    comp = lax.axis_index("comp")
    tile = lax.axis_index("tile")
    even = tile % 2 == 0

    cs = pl.multiple_of((1 - comp) * (COLS - 128), 128)
    os_ = pl.multiple_of((1 - comp) * (OCOLS - 128), 128)
    loads = [
        pltpu.make_async_copy(x.at[:, :, :, pl.ds(cs, 128)], xt, sems.at[1]),
        pltpu.make_async_copy(flow.at[:, :, :, pl.ds(os_, 128)], ft, sems.at[2]),
        pltpu.make_async_copy(warm.at[:, pl.ds(os_, 128)], wt, sems.at[3]),
    ]

    def rows_to(pay, rows, edge, oedge, sem):
        out = []
        for d in range(2):
            for f in range(3):
                out.append((x.at[f, :, rows[d], :], pay.at[pl.ds((d * 3 + f) * 16, 16), :]))
        for f in range(3):
            out.append((x.at[f, 0, rows[2], :], pay.at[104 + f, :]))
        out.append((ex.at[edge, :], pay.at[107, :]))
        out.append((air.at[edge, :], pay.at[108, :]))
        for k in range(2):
            cols = pl.ds(k * OCOLS, OCOLS)
            out.append((flow.at[k, pl.ds(0, 8), oedge, :], pay.at[pl.ds(96, 8), cols]))
            for lv in (8, 9):
                out.append((flow.at[k, lv, oedge, :], pay.at[101 + lv, cols]))
        out.append((warm.at[oedge, :], pay.at[111, pl.ds(0, OCOLS)]))
        return [pltpu.make_async_copy(a, b, sem) for a, b in out]

    top = ((0, 1, 2), 0, 0)
    bottom = ((15, 14, 13), 15, 7)

    @pl.when(even)
    def _():
        for c in rows_to(pay_b, *top, sems.at[0]) + rows_to(pay_a, *bottom, sems.at[0]):
            c.start()

    @pl.when(jnp.logical_not(even))
    def _():
        for c in rows_to(pay_b, *bottom, sems.at[0]) + rows_to(pay_a, *top, sems.at[0]):
            c.start()

    for c in loads:
        c.start()
    for c in loads:
        c.wait()
    lane = lanes()
    back = 1 - comp
    for rt in range(2):
        acc = jnp.zeros((8, 128), F32)
        for g in range(48):
            v = xt[g // 16, g % 16, rt * 8 : rt * 8 + 8, :]
            v = pltpu.roll(v, (2 * g + 2 * back) % 128, 1)
            acc = jnp.where(lane // 2 == g, v, acc)
        packed[rt * 8 : rt * 8 + 8, :] = acc
    acc = jnp.zeros((8, 128), F32)
    for g in range(21):
        v = ft[g // 10, g % 10] if g < 20 else wt[...]
        v = pltpu.roll(v, g + back, 1)
        acc = jnp.where(lane == g, v, acc)
    packed[16:24, :] = acc
    swp[...] = packed[...]
    first = jnp.where(even, 0, 8)
    dg_b[...] = packed[pl.ds(pl.multiple_of(first, 8), 8), :]
    dg_a[...] = packed[pl.ds(pl.multiple_of(8 - first, 8), 8), :]
    for c in rows_to(pay_b, *top, sems.at[0]) + rows_to(pay_a, *bottom, sems.at[0]):
        c.wait()


def pack(x, ex, air, flow, warm):
    vm = pl.BlockSpec(memory_space=pltpu.VMEM)
    sds = jax.ShapeDtypeStruct
    return pl.pallas_call(
        pack_kernel,
        out_shape=(
            sds((112, COLS), F32),
            sds((112, COLS), F32),
            sds((24, 128), F32),
            sds((8, 128), F32),
            sds((8, 128), F32),
        ),
        in_specs=[ANY] * 5,
        out_specs=(ANY, ANY, vm, vm, vm),
        scratch_shapes=[
            pltpu.VMEM((3, LEV, ROWS, 128), F32),
            pltpu.VMEM((2, OLEV, OROWS, 128), F32),
            pltpu.VMEM((OROWS, 128), F32),
            pltpu.VMEM((24, 128), F32),
            pltpu.SemaphoreType.DMA((4,)),
        ],
        compiler_params=pltpu.CompilerParams(vmem_limit_bytes=48 << 20),
        name="pack",
    )(x, ex, air, flow, warm)


def substep(src, level, tiles, lane, sub, store):
    up_l = jnp.maximum(level - 1, 0)
    dn_l = jnp.minimum(level + 1, LEV - 1)
    c, east, west, down, up = {}, {}, {}, {}, {}

    def need(lt):
        lt = lt % 9
        if (0, 0, lt) in c:
            return
        for f in range(3):
            for rt in range(3):
                v = src[f, level, rt * 8 : rt * 8 + 8, lt * 128 : lt * 128 + 128]
                c[f, rt, lt] = v
                if rt in tiles:
                    east[f, rt, lt] = pltpu.roll(v, 1, 1)
                    west[f, rt, lt] = pltpu.roll(v, 127, 1)
                up[f, rt, lt] = pltpu.roll(v, 1, 0)
                down[f, rt, lt] = pltpu.roll(v, 7, 0)

    need(8)
    need(0)
    for lt in range(9):
        need(lt + 1)
        for rt in tiles:
            left, right, prev, nxt, vert, four = {}, {}, {}, {}, {}, {}
            for f in range(3):
                left[f] = jnp.where(lane == 0, east[f, rt, (lt - 1) % 9], east[f, rt, lt])
                right[f] = jnp.where(lane == 127, west[f, rt, (lt + 1) % 9], west[f, rt, lt])
                prev[f] = jnp.where(sub == 0, up[f, (rt - 1) % 3, lt], up[f, rt, lt])
                nxt[f] = jnp.where(sub == 7, down[f, (rt + 1) % 3, lt], down[f, rt, lt])
                rows, cols = slice(rt * 8, rt * 8 + 8), slice(lt * 128, lt * 128 + 128)
                vert[f] = src[f, up_l, rows, cols] + src[f, dn_l, rows, cols]
                four[f] = 2.0 * ((left[f] + right[f]) + (prev[f] + nxt[f])) + vert[f]
            e = 0.06 * c[1, rt, lt] + 0.1 * (four[0] + (left[2] - right[2]))
            n = 0.1 * (four[1] + (prev[2] - nxt[2])) - 0.06 * c[0, rt, lt]
            h = 0.1 * (four[2] + (left[0] - right[0]) + (prev[1] - nxt[1]))
            store(rt, lt, (e, n, h))


def main_kernel(
    x, ex, air, flow, warm, water, part, tally, wgt, pay_a, pay_b, swp, dg_a, dg_b,
    out_x, out_flow, out_warm,
    s0, s1, s2, fl, coef, blocks, wv, res, oc, mask, of, ow, small, xsem, sems, wsem, osem,
):
    comp = lax.axis_index("comp")
    tile = lax.axis_index("tile")
    even = tile % 2 == 0
    lane, sub = lanes(), sublanes()

    wcopy = pltpu.make_async_copy(wgt, wv, wsem)
    xcopies = [
        pltpu.make_async_copy(x.at[f], s0.at[f, :, pl.ds(0, 16), pl.ds(0, COLS)], xsem.at[f])
        for f in range(3)
    ]
    for c in xcopies:
        c.start()

    def halo(pay, rows, third, sem):
        out = []
        for d in range(2):
            for f in range(3):
                out.append(
                    (pay.at[pl.ds((d * 3 + f) * 16, 16), :], s0.at[f, :, rows[d], pl.ds(0, COLS)])
                )
        for f in range(3):
            out.append((pay.at[104 + f, :], s0.at[f, 0, rows[2], pl.ds(0, COLS)]))
        to = pl.ds(0, OCOLS)
        for k in range(2):
            out.append((pay.at[107 + k, :], coef.at[k, rows[0], :]))
            cols = pl.ds(k * OCOLS, OCOLS)
            out.append((pay.at[pl.ds(96, 8), cols], oc.at[pl.ds(k * 10, 8), third, to]))
            for lv in (8, 9):
                out.append((pay.at[101 + lv, cols], oc.at[k * 10 + lv, third, to]))
        out.append((pay.at[111, to], oc.at[20, third, to]))
        return [pltpu.make_async_copy(a, b, sem) for a, b in out]

    above = ((23, 22, 21), 8)
    below = ((16, 17, 18), 15)
    smalls = [
        pltpu.make_async_copy(swp, small.at[pl.ds(0, 24), :], sems.at[1]),
        pltpu.make_async_copy(dg_a, small.at[pl.ds(24, 8), :], sems.at[1]),
        pltpu.make_async_copy(dg_b, small.at[pl.ds(32, 8), :], sems.at[1]),
    ]
    own = [
        pltpu.make_async_copy(ex, coef.at[0, pl.ds(0, 16), :], sems.at[2]),
        pltpu.make_async_copy(air, coef.at[1, pl.ds(0, 16), :], sems.at[2]),
        pltpu.make_async_copy(flow.at[0], oc.at[pl.ds(0, 10), pl.ds(0, 8), pl.ds(0, OCOLS)], sems.at[2]),
        pltpu.make_async_copy(flow.at[1], oc.at[pl.ds(10, 10), pl.ds(0, 8), pl.ds(0, OCOLS)], sems.at[2]),
        pltpu.make_async_copy(warm, oc.at[20, pl.ds(0, 8), pl.ds(0, OCOLS)], sems.at[2]),
        pltpu.make_async_copy(water, mask, sems.at[2]),
    ]

    @pl.when(even)
    def _():
        for c in halo(pay_b, *above, sems.at[0]) + halo(pay_a, *below, sems.at[0]):
            c.start()

    @pl.when(jnp.logical_not(even))
    def _():
        for c in halo(pay_a, *above, sems.at[0]) + halo(pay_b, *below, sems.at[0]):
            c.start()

    for c in smalls + own:
        c.start()
    wcopy.start()

    for c in smalls:
        c.wait()
    has_above = tile > 0
    has_below = tile < lax.axis_size("tile") - 1
    row_ok = jnp.where(sub >= 4, has_above.astype(jnp.int32), has_below.astype(jnp.int32)) > 0
    edge2 = jnp.where(comp == 0, lane, 127 - lane) < 2
    edge1 = jnp.where(comp == 0, lane, 127 - lane) < 1
    top_dg = jnp.where(even, 32, 24)
    corner = jnp.where(
        sub < 4,
        small[pl.ds(pl.multiple_of(56 - top_dg, 8), 8), :],
        small[pl.ds(pl.multiple_of(top_dg, 8), 8), :],
    )
    for g in range(48):
        shift = (128 - 2 * g + 126 * comp) % 128
        for rt in range(3):
            v = small[rt * 8 : rt * 8 + 8, :] if rt < 2 else corner
            ok = edge2 if rt < 2 else edge2 & row_ok
            s0[g // 16, g % 16, rt * 8 : rt * 8 + 8, COLS:WIDE] = jnp.where(
                ok, pltpu.roll(v, shift, 1), 0.0
            )

    for c in xcopies:
        c.wait()
    for c in halo(pay_b, *above, sems.at[0]) + halo(pay_a, *below, sems.at[0]):
        c.wait()
    for c in own:
        c.wait()

    @pl.when(jnp.logical_not(has_above & has_below))
    def _():
        def clear(g, _):
            for lt in range(8):
                cols = slice(lt * 128, lt * 128 + 128)
                for f in range(3):
                    s0[f, g, 16:24, cols] = jnp.where(row_ok, s0[f, g, 16:24, cols], 0.0)
            return 0

        lax.fori_loop(0, LEV, clear, 0)

        def oclear(g, _):
            for lt in range(4):
                cols = slice(lt * 128, lt * 128 + 128)
                keep = jnp.where(sub < 4, has_above.astype(jnp.int32), has_below.astype(jnp.int32)) > 0
                oc[g, 8:16, cols] = jnp.where(keep, oc[g, 8:16, cols], 0.0)
            return 0

        lax.fori_loop(0, 21, oclear, 0)

    def first(level, _):
        def store(rt, lt, new):
            rows, cols = slice(rt * 8, rt * 8 + 8), slice(lt * 128, lt * 128 + 128)
            for f in range(3):
                v = new[f]
                if lt == 8:
                    v = jnp.where(edge1 & row_ok if rt == 2 else edge1, v, 0.0)
                elif rt == 2:
                    v = jnp.where(row_ok, v, 0.0)
                s1[f, level, rows, cols] = v

        substep(s0, level, (0, 1, 2), lane, sub, store)
        return 0

    lax.fori_loop(0, LEV, first, 0)

    def out_copy(level):
        return pltpu.make_async_copy(s2.at[:, level], out_x.at[:, level], osem)

    def put_level0(rt, lt, new):
        rows, cols = slice(rt * 8, rt * 8 + 8), slice(lt * 128, lt * 128 + 128)
        if lt == 8:
            return
        for f in range(3):
            if rt < 2:
                s2[f, 0, rows, cols] = new[f]
        e, n, h = new
        mult = coef[0, rows, cols] * jnp.sqrt(e * e + n * n + 0.25)
        for f, v in enumerate((mult * e, mult * n, mult * (coef[1, rows, cols] - h))):
            hi = v.astype(jnp.bfloat16).astype(F32)
            blocks[pl.ds(rt * 512 + lt * 8 + f, 8, stride=64), :] = hi
            blocks[pl.ds(rt * 512 + lt * 8 + 3 + f, 8, stride=64), :] = v - hi
        blocks[pl.ds(rt * 512 + lt * 8 + 6, 8, stride=64), :] = jnp.ones((8, 128), F32)
        blocks[pl.ds(rt * 512 + lt * 8 + 7, 8, stride=64), :] = jnp.zeros((8, 128), F32)

    substep(s1, 0, (0, 1, 2), lane, sub, put_level0)
    out_copy(0).start()

    def second(level, _):
        def store(rt, lt, new):
            if lt == 8:
                return
            rows, cols = slice(rt * 8, rt * 8 + 8), slice(lt * 128, lt * 128 + 128)
            for f in range(3):
                s2[f, level, rows, cols] = new[f]

        substep(s1, level, (0, 1), lane, sub, store)
        out_copy(level).start()
        return 0

    lax.fori_loop(1, LEV, second, 0)

    wcopy.wait()
    base = tile * 128

    def remap(g, _):
        live = tally[g]
        parts = []
        for s in range(4):
            p = part[g, s] - base
            p = jnp.where(p < 0, p + 192, p)
            row = pl.multiple_of(p * 8, 8)
            v = blocks[pl.ds(row, 8), :]
            parts.append(v * jnp.where(s < live, 1.0, 0.0))
        lhs = jnp.concatenate(parts, axis=1).astype(jnp.bfloat16)
        rhs = wv[g].reshape(512, 128)
        res[pl.ds(pl.multiple_of(g * 8, 8), 8), :] = jnp.dot(lhs, rhs, preferred_element_type=F32)
        return 0

    lax.fori_loop(0, 32, remap, 0, unroll=4)

    def unpack_ocean():
        for g in range(21):
            shift = (128 - g + 127 * comp) % 128
            v = pltpu.roll(small[16:24, :], shift, 1)
            oc[g, 0:8, OCOLS:OWIDE] = jnp.where(edge1, v, 0.0)

    unpack_ocean()

    def around(g, lt):
        cols = slice(lt * 128, lt * 128 + 128)
        c = oc[g, 0:8, cols]
        hv = oc[g, 8:16, cols]
        lo, hi = (lt - 1) % 5, lt + 1
        left = jnp.where(lane == 0, pltpu.roll(oc[g, 0:8, lo * 128 : lo * 128 + 128], 1, 1), pltpu.roll(c, 1, 1))
        right = jnp.where(lane == 127, pltpu.roll(oc[g, 0:8, hi * 128 : hi * 128 + 128], 127, 1), pltpu.roll(c, 127, 1))
        prev = jnp.where(sub == 0, hv, pltpu.roll(c, 1, 0))
        nxt = jnp.where(sub == 7, hv, pltpu.roll(c, 7, 0))
        return c, left, right, prev, nxt

    for lt in range(4):
        cols = slice(lt * 128, lt * 128 + 128)
        m = mask[:, cols].astype(F32)
        den = res[pl.ds(lt * 8 + 6, 8, stride=32), :]
        rem = [
            (res[pl.ds(lt * 8 + f, 8, stride=32), :] + res[pl.ds(lt * 8 + f + 3, 8, stride=32), :]) / den
            for f in range(3)
        ]
        for k in range(2):
            for lv in range(10):
                g = k * 10 + lv
                c, left, right, prev, nxt = around(g, lt)
                other = oc[(1 - k) * 10 + lv, 0:8, cols]
                vert = oc[k * 10 + max(lv - 1, 0), 0:8, cols] + oc[k * 10 + min(lv + 1, 9), 0:8, cols]
                v = 0.2 * ((left + right) + (prev + nxt)) + 0.1 * vert
                v = v + (0.06 if k == 0 else -0.06) * other
                if lv == 0:
                    v = v + 0.2 * rem[k]
                of[k, lv, :, cols] = m * v
        c, left, right, prev, nxt = around(20, lt)
        lap = (left + right) + (prev + nxt) - 4.0 * c
        carried = oc[0, 0:8, cols] * (0.5 * (right - left)) + oc[10, 0:8, cols] * (0.5 * (nxt - prev))
        ow[:, cols] = c + (m * 0.2) * (rem[2] - carried + 0.5 * lap)
    tail = [
        pltpu.make_async_copy(of, out_flow, sems.at[3]),
        pltpu.make_async_copy(ow, out_warm, sems.at[3]),
    ]
    for c in tail:
        c.start()
    for c in tail:
        c.wait()
    lax.fori_loop(0, LEV, lambda l, _: (out_copy(l).wait(), 0)[1], 0)


def advance_all(x, ex, air, flow, warm, water, part, tally, wgt, halos):
    sds = jax.ShapeDtypeStruct
    return pl.pallas_call(
        main_kernel,
        out_shape=(sds(x.shape, F32), sds(flow.shape, F32), sds(warm.shape, F32)),
        in_specs=[ANY] * 6 + [SMEM] * 2 + [ANY] * 6,
        out_specs=(ANY, ANY, ANY),
        scratch_shapes=[
            pltpu.VMEM((3, LEV, 24, WIDE), F32),
            pltpu.VMEM((3, LEV, 24, WIDE), F32),
            pltpu.VMEM((3, LEV, ROWS, COLS), F32),
            pltpu.VMEM((8, 128), F32),
            pltpu.VMEM((2, 24, COLS), F32),
            pltpu.VMEM((24 * 64, 128), F32),
            pltpu.VMEM((32, 4, 128, 128), jnp.bfloat16),
            pltpu.VMEM((256, 128), F32),
            pltpu.VMEM((21, 16, OWIDE), F32),
            pltpu.VMEM((OROWS, OCOLS), jnp.int32),
            pltpu.VMEM((2, OLEV, OROWS, OCOLS), F32),
            pltpu.VMEM((OROWS, OCOLS), F32),
            pltpu.VMEM((40, 128), F32),
            pltpu.SemaphoreType.DMA((3,)),
            pltpu.SemaphoreType.DMA((4,)),
            pltpu.SemaphoreType.DMA,
            pltpu.SemaphoreType.DMA,
        ],
        compiler_params=pltpu.CompilerParams(vmem_limit_bytes=48 << 20),
        name="advance_all",
    )(x, ex, air, flow, warm, water, part, tally, wgt, *halos)


def exchange(pay_a, pay_b, swp, dg_a, dg_b):
    tiles = lax.axis_size("tile")
    pair_a = [t ^ 1 for t in range(tiles)]
    pair_b = [t if t in (0, tiles - 1) else (t - 1 if t % 2 == 0 else t + 1) for t in range(tiles)]

    def straight(v, pair):
        return lax.ppermute(v, "tile", list(enumerate(pair)))

    def diagonal(v, pair):
        perm = [(c * tiles + t, (1 - c) * tiles + p) for c in range(2) for t, p in enumerate(pair)]
        return lax.ppermute(v, ("comp", "tile"), perm)

    got_b = straight(pay_b, pair_b)
    got_a = straight(pay_a, pair_a)
    return (
        got_a,
        got_b,
        lax.ppermute(swp, "comp", [(0, 1), (1, 0)]),
        diagonal(dg_a, pair_a),
        diagonal(dg_b, pair_b),
    )


def shards(x, ex, air, flow, warm, water, part, tally, wgt):
    halos = exchange(*pack(x, ex, air, flow, warm))
    return advance_all(x, ex, air, flow, warm, water, part, tally, wgt, halos)


def solution(mesh):
    placed = (
        P(None, None, "tile", "comp"),
        P("tile", "comp"),
        P("tile", "comp"),
        P(None, None, "tile", "comp"),
        P("tile", "comp"),
        P("tile", "comp"),
        P(("comp", "tile"), None),
        P(("comp", "tile")),
        P(("comp", "tile"), None, None, None),
    )
    return jax.shard_map(
        shards,
        mesh=mesh,
        in_specs=placed,
        out_specs=(P(None, None, "tile", "comp"), P(None, None, "tile", "comp"), P("tile", "comp")),
        check_vma=False,
    )
```

```python
import functools

import jax
import jax.numpy as jnp
from jax import lax
from jax.experimental import pallas as pl
from jax.experimental.pallas import tpu as pltpu
from jax.sharding import PartitionSpec as P

F32 = jnp.float32
VMEM_ALL = 63 << 20
LEV, ROWS, COLS = 16, 16, 1024
OLEV, OROWS, OCOLS = 10, 8, 512
WIDE = COLS + 128
OWIDE = OCOLS + 128
ANY = pl.BlockSpec(memory_space=pl.ANY)
SMEM = pl.BlockSpec(memory_space=pltpu.SMEM)


def lanes():
    return lax.broadcasted_iota(jnp.int32, (8, 128), 1)


def sublanes():
    return lax.broadcasted_iota(jnp.int32, (8, 128), 0)


def sweep(src, level, up_l, dn_l, rts, lts, wrap, edge, store):
    lane, sub = lanes(), sublanes()
    c, east, west, down, up = {}, {}, {}, {}, {}
    every = range(3) if wrap else rts
    nl = 9 if wrap else 8
    nr = len(every)

    def need(lt):
        if (0, every[0], lt) in c:
            return
        for f in range(3):
            for rt in every:
                v = src[f, level, rt * 8 : rt * 8 + 8, lt * 128 : lt * 128 + 128]
                c[f, rt, lt] = v
                if rt in rts:
                    east[f, rt, lt] = pltpu.roll(v, 1, 1)
                    west[f, rt, lt] = pltpu.roll(v, 127, 1)
                up[f, rt, lt] = pltpu.roll(v, 1, 0)
                down[f, rt, lt] = pltpu.roll(v, 7, 0)

    if wrap:
        need(8)
    need(0)
    for lt in lts:
        if wrap or lt < nl - 1:
            need((lt + 1) % nl)
        for rt in rts:
            inner = {
                "left": wrap or lt > 0,
                "right": wrap or lt < nl - 1,
                "prev": wrap or rt > 0,
                "next": wrap or rt < nr - 1,
            }
            out = {k: None if v else edge(k, rt, lt) for k, v in inner.items()}
            left, right, prev, nxt, four = {}, {}, {}, {}, {}
            for f in range(3):
                o = {k: out[k][f] if out[k] is not None else None for k in out}
                if inner["left"]:
                    o["left"] = east[f, rt, (lt - 1) % nl]
                if inner["right"]:
                    o["right"] = west[f, rt, (lt + 1) % nl]
                if inner["prev"]:
                    o["prev"] = up[f, (rt - 1) % nr, lt]
                if inner["next"]:
                    o["next"] = down[f, (rt + 1) % nr, lt]
                left[f] = jnp.where(lane == 0, o["left"], east[f, rt, lt])
                right[f] = jnp.where(lane == 127, o["right"], west[f, rt, lt])
                prev[f] = jnp.where(sub == 0, o["prev"], up[f, rt, lt])
                nxt[f] = jnp.where(sub == 7, o["next"], down[f, rt, lt])
                rows, cols = slice(rt * 8, rt * 8 + 8), slice(lt * 128, lt * 128 + 128)
                vert = src[f, up_l, rows, cols] + src[f, dn_l, rows, cols]
                four[f] = 2.0 * ((left[f] + right[f]) + (prev[f] + nxt[f])) + vert
            e = 0.06 * c[1, rt, lt] + 0.1 * (four[0] + (left[2] - right[2]))
            n = 0.1 * (four[1] + (prev[2] - nxt[2])) - 0.06 * c[0, rt, lt]
            h = 0.1 * (four[2] + (left[0] - right[0]) + (prev[1] - nxt[1]))
            store(rt, lt, (e, n, h))


def sideways(v, sign):
    e, n, h = v
    return (0.1 * (2.0 * e + sign * h), 0.2 * n, 0.1 * (2.0 * h + sign * e))


def upright(v, sign):
    e, n, h = v
    return (0.2 * e, 0.1 * (2.0 * n + sign * h), 0.1 * (2.0 * h + sign * n))


def neighbours():
    tile = lax.axis_index("tile")
    return tile > 0, tile < lax.axis_size("tile") - 1


def share(early):
    place = lax.axis_index("tile") % 16
    cut = jnp.where(place == 0, LEV, jnp.where(place == 1, LEV // 2, 0))
    return (0, cut) if early else (cut, LEV)


def own_work(x, s1, s2, out_x, rb, cb, sem, ready, lo, hi):
    comp = lax.axis_index("comp")
    has_above, has_below = neighbours()
    zero = jnp.zeros((8, 128), F32)

    def first(level, _):
        ready(level)

        def store(rt, lt, new):
            for f in range(3):
                s1[f, level, rt * 8 : rt * 8 + 8, lt * 128 : lt * 128 + 128] = new[f]

        dn = jnp.minimum(level + 1, LEV - 1)
        sweep(x, level, jnp.maximum(level - 1, 0), dn, (0, 1), range(8), False, lambda *a: (zero,) * 3, store)
        return 0

    lax.fori_loop(jnp.maximum(lo - 1, 0), jnp.minimum(hi + 1, LEV), first, 0)
    gain = {
        "left": comp.astype(F32),
        "right": (1 - comp).astype(F32),
        "prev": has_above.astype(F32),
        "next": has_below.astype(F32),
    }

    def out_copy(level):
        return pltpu.make_async_copy(s2.at[:, level], out_x.at[:, level], sem)

    def second(level, _):
        def edge(kind, rt, lt):
            v = [x[f, level, rt * 8 : rt * 8 + 8, lt * 128 : lt * 128 + 128] for f in range(3)]
            put = sideways if kind in ("left", "right") else upright
            return [gain[kind] * w for w in put(v, -1.0 if kind in ("left", "prev") else 1.0)]

        def store(rt, lt, new):
            for f in range(3):
                s2[f, level, rt * 8 : rt * 8 + 8, lt * 128 : lt * 128 + 128] = new[f]

        dn = jnp.minimum(level + 1, LEV - 1)
        sweep(s1, level, jnp.maximum(level - 1, 0), dn, (0, 1), range(8), False, edge, store)
        out_copy(level).start()
        return 0

    lax.fori_loop(lo, hi, second, 0)
    es = pl.multiple_of((1 - comp) * (COLS - 128), 128)

    def kept(half):
        some = pl.ds(half * 8, 8)
        out = [pltpu.make_async_copy(s2.at[:, some, :, pl.ds(es, 128)], cb.at[:, some], sem)]
        for k, r in enumerate((0, 1, 15, 14)):
            for f in range(3):
                to = rb.at[pl.ds((k * 3 + f) * 16 + half * 8, 8), :]
                out.append(pltpu.make_async_copy(s2.at[f, some, r, :], to, sem))
        return out

    for half in range(2):

        @pl.when((lo <= half * 8) & (half * 8 < hi))
        def _():
            for c in kept(half):
                c.start()

    for half in range(2):

        @pl.when((lo <= half * 8) & (half * 8 < hi))
        def _():
            for c in kept(half):
                c.wait()

    lax.fori_loop(lo, hi, lambda l, _: (out_copy(l).wait(), 0)[1], 0)


def pack_kernel(
    x_in, ex_in, air_in, flow_in, warm_in,
    pay_up, pay_dn, swp,
    x, ex, air, flow, warm, packed, sems,
):
    comp = lax.axis_index("comp")
    cs = pl.multiple_of((1 - comp) * (COLS - 128), 128)
    os_ = pl.multiple_of((1 - comp) * (OCOLS - 128), 128)
    loads = [
        pltpu.make_async_copy(a, b, sems.at[1])
        for a, b in ((x_in, x), (ex_in, ex), (air_in, air), (flow_in, flow), (warm_in, warm))
    ]
    for c in loads:
        c.start()

    def rows_to(pay, rows, edge, oedge, sem):
        out = []
        for d in range(2):
            for f in range(3):
                out.append((x.at[f, :, rows[d], :], pay.at[pl.ds((d * 3 + f) * 16, 16), :]))
        for f in range(3):
            out.append((x.at[f, 0, rows[2], :], pay.at[104 + f, :]))
        out.append((ex.at[edge, :], pay.at[107, :]))
        out.append((air.at[edge, :], pay.at[108, :]))
        for k in range(2):
            cols = pl.ds(k * OCOLS, OCOLS)
            out.append((flow.at[k, pl.ds(0, 8), oedge, :], pay.at[pl.ds(96, 8), cols]))
            for lv in (8, 9):
                out.append((flow.at[k, lv, oedge, :], pay.at[101 + lv, cols]))
        out.append((warm.at[oedge, :], pay.at[111, pl.ds(0, OCOLS)]))
        return [pltpu.make_async_copy(a, b, sem) for a, b in out]

    top = ((0, 1, 2), 0, 0)
    bottom = ((15, 14, 13), 15, 7)

    for c in loads:
        c.wait()

    sends = rows_to(pay_up, *bottom, sems.at[0]) + rows_to(pay_dn, *top, sems.at[0])
    for c in sends:
        c.start()

    lane = lanes()
    back = 1 - comp
    for rt in range(2):
        acc = jnp.zeros((8, 128), F32)
        for g in range(48):
            v = x[g // 16, g % 16, rt * 8 : rt * 8 + 8, pl.ds(cs, 128)]
            v = pltpu.roll(v, (2 * g + 2 * back) % 128, 1)
            acc = jnp.where(lane // 2 == g, v, acc)
        packed[rt * 8 : rt * 8 + 8, :] = acc
    acc = jnp.zeros((8, 128), F32)
    for g in range(21):
        v = flow[g // 10, g % 10, :, pl.ds(os_, 128)] if g < 20 else warm[:, pl.ds(os_, 128)]
        v = pltpu.roll(v, g + back, 1)
        acc = jnp.where(lane == g, v, acc)
    packed[16:24, :] = acc
    swp[...] = packed[...]
    corners = [
        pltpu.make_async_copy(packed.at[pl.ds(8, 8), :], pay_up.at[pl.ds(112, 8), pl.ds(0, 128)], sems.at[0]),
        pltpu.make_async_copy(packed.at[pl.ds(0, 8), :], pay_dn.at[pl.ds(112, 8), pl.ds(0, 128)], sems.at[0]),
    ]
    for c in corners:
        c.start()
    for c in sends + corners:
        c.wait()


KEPT = ((3, LEV, ROWS, COLS), (192, COLS), (3, LEV, ROWS, 128))
STATE = pltpu.VMEM((3, LEV, ROWS, COLS), F32)


def pack(x, ex, air, flow, warm):
    vm = pl.BlockSpec(memory_space=pltpu.VMEM)
    sds = jax.ShapeDtypeStruct
    return pl.pallas_call(
        pack_kernel,
        out_shape=(
            sds((128, COLS), F32),
            sds((120, COLS), F32),
            sds((24, 128), F32),
        ),
        in_specs=[ANY] * 5,
        out_specs=(ANY, ANY, vm),
        scratch_shapes=[
            STATE,
            pltpu.VMEM((ROWS, COLS), F32),
            pltpu.VMEM((ROWS, COLS), F32),
            pltpu.VMEM((2, OLEV, OROWS, OCOLS), F32),
            pltpu.VMEM((OROWS, OCOLS), F32),
            pltpu.VMEM((24, 128), F32),
            pltpu.SemaphoreType.DMA((2,)),
        ],
        compiler_params=pltpu.CompilerParams(vmem_limit_bytes=VMEM_ALL),
        name="pack",
    )(x, ex, air, flow, warm)


def own_kernel(early, passed, x_in, *refs):
    out_x, rb, cb = refs[passed : passed + 3]
    x, s1, s2, sem, xsem = refs[-5:]
    lo, hi = share(early)

    @pl.when(lo < hi)
    def _():
        def load(level):
            return pltpu.make_async_copy(x_in.at[:, level], x.at[:, level], xsem.at[level])

        begin = jnp.maximum(lo - 2, 0)
        lax.fori_loop(begin, jnp.minimum(hi + 2, LEV), lambda l, _: (load(l).start(), 0)[1], 0)
        lax.fori_loop(begin, jnp.maximum(lo, 1), lambda l, _: (load(l).wait(), 0)[1], 0)

        def ready(level):
            @pl.when(level < LEV - 1)
            def _():
                load(level + 1).wait()

        own_work(x, s1, s2, out_x, rb, cb, sem, ready, lo, hi)


def own(x, early, passed):
    shapes = [v.shape for v in passed] if not early else [v.shape for v in passed] + list(KEPT)
    aliased = {i + 1: i for i in range(len(passed))}
    return pl.pallas_call(
        functools.partial(own_kernel, early, len(shapes) + len(passed) - 3),
        out_shape=tuple(jax.ShapeDtypeStruct(k, F32) for k in shapes),
        in_specs=[ANY] * (1 + len(passed)),
        out_specs=(ANY,) * len(shapes),
        input_output_aliases=aliased,
        scratch_shapes=[STATE, STATE, STATE, pltpu.SemaphoreType.DMA, pltpu.SemaphoreType.DMA((LEV,))],
        compiler_params=pltpu.CompilerParams(vmem_limit_bytes=VMEM_ALL),
        name="own_early" if early else "own_late",
    )(x, *passed)


def row_terms(near, far, mid, edge, kept, sign):
    lane, sub = lanes(), sublanes()
    zero = jnp.zeros((8, 128), F32)

    def at(ref, f, st, lt):
        return ref[f * 16 + st * 8 : f * 16 + st * 8 + 8, lt * 128 : lt * 128 + 128]

    def full(src, out, put):
        for lt in range(8):
            for st in range(2):
                c, left, right, four = {}, {}, {}, {}
                o = [at(out, f, st, lt) for f in range(3)]
                for f in range(3):
                    c[f] = at(src, f, st, lt)
                    lo = pltpu.roll(at(src, f, st, lt - 1), 1, 1) if lt > 0 else zero
                    hi = pltpu.roll(at(src, f, st, lt + 1), 127, 1) if lt < 7 else zero
                    left[f] = jnp.where(lane == 0, lo, pltpu.roll(c[f], 1, 1))
                    right[f] = jnp.where(lane == 127, hi, pltpu.roll(c[f], 127, 1))
                    other = at(src, f, 1 - st, lt)
                    above = jnp.where(sub == 0, c[f] if st == 0 else pltpu.roll(other, 1, 0), pltpu.roll(c[f], 1, 0))
                    below = jnp.where(sub == 7, c[f] if st == 1 else pltpu.roll(other, 7, 0), pltpu.roll(c[f], 7, 0))
                    four[f] = 2.0 * (left[f] + right[f] + o[f]) + (above + below)
                e = 0.06 * c[1] + 0.1 * (four[0] + (left[2] - right[2]))
                n = 0.1 * (four[1] + sign * o[2]) - 0.06 * c[0]
                h = 0.1 * (four[2] + (left[0] - right[0]) + sign * o[1])
                put(st, lt, (e, n, h))

    def put_edge(st, lt, new):
        for f in range(3):
            edge[f * 16 + st * 8 : f * 16 + st * 8 + 8, lt * 128 : lt * 128 + 128] = new[f]

    full(near, far, put_edge)
    for lt in range(8):
        for st in range(2):
            y = upright([at(near, f, st, lt) for f in range(3)], sign)
            z = upright(y, sign)
            for f in range(3):
                rows, cols = slice(f * 16 + st * 8, f * 16 + st * 8 + 8), slice(lt * 128, lt * 128 + 128)
                mid[rows, cols] = y[f]
                kept[48 + f * 16 + st * 8 : 48 + f * 16 + st * 8 + 8, cols] += z[f]

    def put_kept(st, lt, new):
        for f in range(3):
            kept[f * 16 + st * 8 : f * 16 + st * 8 + 8, lt * 128 : lt * 128 + 128] += new[f]

    full(mid, edge, put_kept)


def column_terms(tiles, comp):
    lane, sub = lanes(), sublanes()
    flip = jnp.where(comp == 1, 1.0, -1.0)
    right_half = comp == 1
    x1, x2 = [[], [], []], [[], [], []]
    for v in tiles:
        w = pltpu.roll(v, 127, 1)
        a = jnp.where(right_half, w, v)
        b = jnp.where(right_half, v, w)
        for f in range(3):
            x1[f].append(pltpu.roll(a, (128 - 32 * f) % 128, 1))
            x2[f].append(pltpu.roll(b, (128 - 32 * f) % 128, 1))

    def lateral(v):
        per_tile = [sideways([v[f][k] for f in range(3)], flip) for k in range(len(v[0]))]
        return [[p[f] for p in per_tile] for f in range(3)]

    def full(c, out):
        res = [[], [], []]
        for rt in range(2):
            prev, nxt, four = {}, {}, {}
            for f in range(3):
                v = c[f][rt]
                p = c[f][2] if rt == 0 else c[f][0]
                q = c[f][1] if rt == 0 else c[f][2]
                prev[f] = jnp.where(sub == 0, pltpu.roll(p, 1, 0), pltpu.roll(v, 1, 0))
                nxt[f] = jnp.where(sub == 7, pltpu.roll(q, 7, 0), pltpu.roll(v, 7, 0))
                above = jnp.where(lane < 2, v, pltpu.roll(v, 2, 1))
                below = jnp.where(lane >= 30, v, pltpu.roll(v, 126, 1))
                four[f] = 2.0 * (prev[f] + nxt[f] + out[f][rt]) + (above + below)
            res[0].append(0.06 * c[1][rt] + 0.1 * (four[0] + flip * out[2][rt]))
            res[1].append(0.1 * (four[1] + (prev[2] - nxt[2])) - 0.06 * c[0][rt])
            res[2].append(0.1 * (four[2] + flip * out[0][rt] + (prev[1] - nxt[1])))
        return res

    y = lateral(x1)
    s0 = full(y, full(x1, x2))
    s1 = lateral([[v[0], v[1]] for v in y])
    pairs = []
    for f in range(3):
        row = []
        for rt in range(2):
            a = jnp.where(right_half, s0[f][rt], s1[f][rt])
            b = jnp.where(right_half, s1[f][rt], s0[f][rt])
            row.append(jnp.where(lane % 2 == 0, a, pltpu.roll(b, 1, 1)))
        pairs.append(row)
    return pairs


def rows_kernel(pay_up, pay_dn, x_own, rb, out_x, ke, halo_rows, mid, edge, kept, sems):
    comp = lax.axis_index("comp")
    loads = [
        pltpu.make_async_copy(rb, kept, sems.at[0]),
        pltpu.make_async_copy(pay_up.at[pl.ds(0, 96), :], halo_rows.at[0], sems.at[0]),
        pltpu.make_async_copy(pay_dn.at[pl.ds(0, 96), :], halo_rows.at[1], sems.at[0]),
    ]
    for c in loads:
        c.start()
    for c in loads:
        c.wait()
    rest = pl.multiple_of(comp * 128, 128)
    es = pl.multiple_of((1 - comp) * (COLS - 128), 128)
    puts = [
        pltpu.make_async_copy(
            kept.at[pl.ds((k * 3 + f) * 16, 16), pl.ds(rest, COLS - 128)],
            out_x.at[f, :, r, pl.ds(rest, COLS - 128)],
            sems.at[1],
        )
        for k, r in enumerate((0, 1, 15, 14))
        for f in range(3)
    ]
    for side, there in enumerate(neighbours()):

        @pl.when(there)
        def _():
            rows = halo_rows.at[side]
            row_terms(
                rows.at[pl.ds(0, 48)], rows.at[pl.ds(48, 48)], mid, edge,
                kept.at[pl.ds(side * 96, 96)], 1.0 if side == 0 else -1.0,
            )

        for c in puts[side * 6 : side * 6 + 6]:
            c.start()
    puts.append(pltpu.make_async_copy(kept.at[:, pl.ds(es, 128)], ke, sems.at[1]))
    puts[-1].start()
    for c in puts:
        c.wait()


def rows(pay_up, pay_dn, x_own, rb):
    sds = jax.ShapeDtypeStruct
    return pl.pallas_call(
        rows_kernel,
        out_shape=(sds(x_own.shape, F32), sds((192, 128), F32)),
        in_specs=[ANY] * 4,
        out_specs=(ANY, ANY),
        input_output_aliases={2: 0},
        scratch_shapes=[
            pltpu.VMEM((2, 96, COLS), F32),
            pltpu.VMEM((48, COLS), F32),
            pltpu.VMEM((48, COLS), F32),
            pltpu.VMEM((192, COLS), F32),
            pltpu.SemaphoreType.DMA((2,)),
        ],
        compiler_params=pltpu.CompilerParams(vmem_limit_bytes=VMEM_ALL),
        name="rows",
    )(pay_up, pay_dn, x_own, rb)


def final_kernel(
    x, ex, air, flow, warm, water, part, tally, wgt, pay_up, pay_dn, swp, x_own, ke, cb,
    out_x, out_flow, out_warm,
    s0, s1, kept, cbv, cbo, coef, blocks, wv, res, oc, mask, of, ow, small, sems,
):
    comp = lax.axis_index("comp")
    tile = lax.axis_index("tile")
    lane, sub = lanes(), sublanes()
    has_above, has_below = neighbours()

    def halo(pay, rows, third):
        out = []
        for d in range(2):
            for f in range(3):
                for lv in range(3 - d):
                    out.append((pay.at[(d * 3 + f) * 16 + lv, :], s0.at[f, lv, rows[d], pl.ds(0, COLS)]))
        for f in range(3):
            out.append((pay.at[104 + f, :], s0.at[f, 0, rows[2], pl.ds(0, COLS)]))
        to = pl.ds(0, OCOLS)
        for k in range(2):
            out.append((pay.at[107 + k, :], coef.at[k, rows[0], :]))
            cols = pl.ds(k * OCOLS, OCOLS)
            out.append((pay.at[pl.ds(96, 8), cols], oc.at[pl.ds(k * 10, 8), third, to]))
            for lv in (8, 9):
                out.append((pay.at[101 + lv, cols], oc.at[k * 10 + lv, third, to]))
        out.append((pay.at[111, to], oc.at[20, third, to]))
        return [pltpu.make_async_copy(a, b, sems.at[1]) for a, b in out]

    above = ((23, 22, 21), 8)
    below = ((16, 17, 18), 15)
    keeps = [pltpu.make_async_copy(ke, kept, sems.at[2]), pltpu.make_async_copy(cb, cbv, sems.at[2])]
    smalls = [pltpu.make_async_copy(swp, small, sems.at[3])]
    mine = [
        pltpu.make_async_copy(x.at[:, pl.ds(0, 3)], s0.at[:, :, pl.ds(0, 16), pl.ds(0, COLS)], sems.at[4]),
        pltpu.make_async_copy(ex, coef.at[0, pl.ds(0, 16), :], sems.at[4]),
        pltpu.make_async_copy(air, coef.at[1, pl.ds(0, 16), :], sems.at[4]),
        pltpu.make_async_copy(flow.at[0], oc.at[pl.ds(0, 10), pl.ds(0, 8), pl.ds(0, OCOLS)], sems.at[4]),
        pltpu.make_async_copy(flow.at[1], oc.at[pl.ds(10, 10), pl.ds(0, 8), pl.ds(0, OCOLS)], sems.at[4]),
        pltpu.make_async_copy(warm, oc.at[20, pl.ds(0, 8), pl.ds(0, OCOLS)], sems.at[4]),
        pltpu.make_async_copy(water, mask, sems.at[4]),
    ]
    wcopy = pltpu.make_async_copy(wgt, wv, sems.at[5])

    halos = halo(pay_up, *above) + halo(pay_dn, *below)
    for c in halos:
        c.start()
    for c in smalls + mine + keeps + [wcopy]:
        c.start()
    for c in smalls:
        c.wait()

    row_ok = jnp.where(sub >= 4, has_above.astype(jnp.int32), has_below.astype(jnp.int32)) > 0
    row_halo = jnp.where(sub < 4, has_above.astype(jnp.int32), has_below.astype(jnp.int32)) > 0
    edge2 = jnp.where(comp == 0, lane, 127 - lane) < 2
    edge1 = jnp.where(comp == 0, lane, 127 - lane) < 1
    corner = jnp.where(row_ok, small[24:32, :], 0.0)
    for f in range(3):
        for lv in range(3):
            shift = (128 - 2 * (f * 16 + lv) + 126 * comp) % 128
            for rt in range(3):
                v = small[rt * 8 : rt * 8 + 8, :] if rt < 2 else corner
                s0[f, lv, rt * 8 : rt * 8 + 8, COLS:WIDE] = jnp.where(edge2, pltpu.roll(v, shift, 1), 0.0)

    for c in mine:
        c.wait()
    for c in halos:
        c.wait()

    @pl.when(jnp.logical_not(has_above & has_below))
    def _():
        for lt in range(8):
            cols = slice(lt * 128, lt * 128 + 128)
            for f in range(3):
                for lv in range(3):
                    s0[f, lv, 16:24, cols] = jnp.where(row_ok, s0[f, lv, 16:24, cols], 0.0)

        def oclear(g, _):
            for lt in range(4):
                cols = slice(lt * 128, lt * 128 + 128)
                oc[g, 8:16, cols] = jnp.where(row_halo, oc[g, 8:16, cols], 0.0)
            return 0

        lax.fori_loop(0, 21, oclear, 0)

    for level in range(2):

        def put_first(rt, lt, new):
            rows, cols = slice(rt * 8, rt * 8 + 8), slice(lt * 128, lt * 128 + 128)
            for f in range(3):
                v = new[f]
                if lt == 8:
                    v = jnp.where(edge1 & row_ok if rt == 2 else edge1, v, 0.0)
                elif rt == 2:
                    v = jnp.where(row_ok, v, 0.0)
                s1[f, level, rows, cols] = v

        sweep(s0, level, 0, level + 1, range(3), range(9), True, None, put_first)

    def put_flux(rt, lt, new):
        rows, cols = slice(rt * 8, rt * 8 + 8), slice(lt * 128, lt * 128 + 128)
        e, n, h = new
        mult = coef[0, rows, cols] * jnp.sqrt(e * e + n * n + 0.25)
        at = rt * 512 + lt * 8
        for f, v in enumerate((mult * e, mult * n, mult * (coef[1, rows, cols] - h))):
            hi = v.astype(jnp.bfloat16).astype(F32)
            blocks[pl.ds(at + f, 8, stride=64), :] = hi
            blocks[pl.ds(at + 3 + f, 8, stride=64), :] = v - hi
        blocks[pl.ds(at + 6, 8, stride=64), :] = jnp.ones((8, 128), F32)
        blocks[pl.ds(at + 7, 8, stride=64), :] = jnp.zeros((8, 128), F32)

    sweep(s1, 0, 0, 1, range(3), range(8), True, None, put_flux)

    for c in keeps:
        c.wait()
    es = pl.multiple_of((1 - comp) * (COLS - 128), 128)
    pairs = column_terms((small[0:8, :], small[8:16, :], corner), comp)
    own2 = jnp.where(comp == 0, 127 - lane, lane) < 2
    for f in range(3):
        for lv in range(16):
            shift = (128 - 2 * lv + 126 * (1 - comp)) % 128
            for rt in range(2):
                v = cbv[f, lv, rt * 8 : rt * 8 + 8, :]
                for k, at in ((0, 0), (1, 1)) if rt == 0 else ((2, 7), (3, 6)):
                    line = kept[(k * 3 + f) * 16 + lv : (k * 3 + f) * 16 + lv + 1, :]
                    v = jnp.where(sub == at, line, v)
                v = v + jnp.where(own2, pltpu.roll(pairs[f][rt], shift, 1), 0.0)
                cbo[f, lv, rt * 8 : rt * 8 + 8, :] = v
    put_edge = pltpu.make_async_copy(cbo, out_x.at[:, :, :, pl.ds(es, 128)], sems.at[7])
    put_edge.start()

    wcopy.wait()
    base = tile * 128

    def remap(g, _):
        live = tally[g]
        parts = []
        for s in range(4):
            p = part[s, g] - base
            p = jnp.where(p < 0, p + 192, p)
            row = pl.multiple_of(p * 8, 8)
            v = blocks[pl.ds(row, 8), :]
            parts.append(v * jnp.where(s < live, 1.0, 0.0))
        lhs = jnp.concatenate(parts, axis=1).astype(jnp.bfloat16)
        rhs = wv[g].reshape(512, 128)
        res[pl.ds(pl.multiple_of(g * 8, 8), 8), :] = jnp.dot(lhs, rhs, preferred_element_type=F32)
        return 0

    lax.fori_loop(0, 32, remap, 0, unroll=4)

    def unpack_ocean():
        for g in range(21):
            shift = (128 - g + 127 * comp) % 128
            v = pltpu.roll(small[16:24, :], shift, 1)
            oc[g, 0:8, OCOLS:OWIDE] = jnp.where(edge1, v, 0.0)

    unpack_ocean()

    def around(g, lt):
        cols = slice(lt * 128, lt * 128 + 128)
        c = oc[g, 0:8, cols]
        hv = oc[g, 8:16, cols]
        lo, hi = (lt - 1) % 5, lt + 1
        left = jnp.where(lane == 0, pltpu.roll(oc[g, 0:8, lo * 128 : lo * 128 + 128], 1, 1), pltpu.roll(c, 1, 1))
        right = jnp.where(lane == 127, pltpu.roll(oc[g, 0:8, hi * 128 : hi * 128 + 128], 127, 1), pltpu.roll(c, 127, 1))
        prev = jnp.where(sub == 0, hv, pltpu.roll(c, 1, 0))
        nxt = jnp.where(sub == 7, hv, pltpu.roll(c, 7, 0))
        return c, left, right, prev, nxt

    for lt in range(4):
        cols = slice(lt * 128, lt * 128 + 128)
        m = mask[:, cols].astype(F32)
        den = res[pl.ds(lt * 8 + 6, 8, stride=32), :]
        rem = [
            (res[pl.ds(lt * 8 + f, 8, stride=32), :] + res[pl.ds(lt * 8 + f + 3, 8, stride=32), :]) / den
            for f in range(3)
        ]
        for k in range(2):
            for lv in range(10):
                g = k * 10 + lv
                c, left, right, prev, nxt = around(g, lt)
                other = oc[(1 - k) * 10 + lv, 0:8, cols]
                vert = oc[k * 10 + max(lv - 1, 0), 0:8, cols] + oc[k * 10 + min(lv + 1, 9), 0:8, cols]
                v = 0.2 * ((left + right) + (prev + nxt)) + 0.1 * vert
                v = v + (0.06 if k == 0 else -0.06) * other
                if lv == 0:
                    v = v + 0.2 * rem[k]
                of[k, lv, :, cols] = m * v
        c, left, right, prev, nxt = around(20, lt)
        lap = (left + right) + (prev + nxt) - 4.0 * c
        carried = oc[0, 0:8, cols] * (0.5 * (right - left)) + oc[10, 0:8, cols] * (0.5 * (nxt - prev))
        ow[:, cols] = c + (m * 0.2) * (rem[2] - carried + 0.5 * lap)
    tail = [
        pltpu.make_async_copy(of, out_flow, sems.at[8]),
        pltpu.make_async_copy(ow, out_warm, sems.at[8]),
    ]
    for c in tail:
        c.start()
    for c in tail + [put_edge]:
        c.wait()


def final(x, ex, air, flow, warm, water, part, tally, wgt, halos, kept):
    sds = jax.ShapeDtypeStruct
    return pl.pallas_call(
        final_kernel,
        out_shape=(sds(x.shape, F32), sds(flow.shape, F32), sds(warm.shape, F32)),
        in_specs=[ANY] * 6 + [SMEM] * 2 + [ANY] * 7,
        out_specs=(ANY, ANY, ANY),
        input_output_aliases={12: 0},
        scratch_shapes=[
            pltpu.VMEM((3, 3, 24, WIDE), F32),
            pltpu.VMEM((3, 2, 24, WIDE), F32),
            pltpu.VMEM((192, 128), F32),
            pltpu.VMEM((3, LEV, ROWS, 128), F32),
            pltpu.VMEM((3, LEV, ROWS, 128), F32),
            pltpu.VMEM((2, 24, COLS), F32),
            pltpu.VMEM((24 * 64, 128), F32),
            pltpu.VMEM((32, 4, 128, 128), jnp.bfloat16),
            pltpu.VMEM((256, 128), F32),
            pltpu.VMEM((21, 16, OWIDE), F32),
            pltpu.VMEM((OROWS, OCOLS), jnp.int32),
            pltpu.VMEM((2, OLEV, OROWS, OCOLS), F32),
            pltpu.VMEM((OROWS, OCOLS), F32),
            pltpu.VMEM((32, 128), F32),
            pltpu.SemaphoreType.DMA((9,)),
        ],
        compiler_params=pltpu.CompilerParams(vmem_limit_bytes=VMEM_ALL),
        name="final",
    )(x, ex, air, flow, warm, water, part, tally, wgt, *halos, *kept)


def shift(v, step, across):
    tiles = lax.axis_size("tile")
    if not across:
        return lax.ppermute(v, "tile", [(t, (t + step) % tiles) for t in range(tiles)])
    perm = [(c * tiles + t, (1 - c) * tiles + (t + step) % tiles) for c in range(2) for t in range(tiles)]
    return lax.ppermute(v, ("comp", "tile"), perm)


def shards(x, ex, air, flow, warm, water, part, tally, wgt):
    pay_up, pay_dn, swp = pack(x, ex, air, flow, warm)
    got_up = shift(pay_up, 1, False)
    pay_dn, *kept = own(x, True, [pay_dn])
    got_dn = shift(pay_dn, -1, False)
    swp, x_own, rb, cb = own(x, False, [swp, *kept])
    upper = lax.broadcasted_iota(jnp.int32, (8, 128), 0) >= 4
    corner = jnp.where(upper, got_up[112:120, :128], got_dn[112:120, :128])
    got_sw = shift(jnp.concatenate([swp, corner], axis=0), 0, True)
    x_own, ke = rows(got_up, got_dn, x_own, rb)
    return final(x, ex, air, flow, warm, water, part.T, tally, wgt, (got_up, got_dn, got_sw), (x_own, ke, cb))


def solution(mesh):
    placed = (
        P(None, None, "tile", "comp"),
        P("tile", "comp"),
        P("tile", "comp"),
        P(None, None, "tile", "comp"),
        P("tile", "comp"),
        P("tile", "comp"),
        P(("comp", "tile"), None),
        P(("comp", "tile")),
        P(("comp", "tile"), None, None, None),
    )
    return jax.shard_map(
        shards,
        mesh=mesh,
        in_specs=placed,
        out_specs=(P(None, None, "tile", "comp"), P(None, None, "tile", "comp"), P("tile", "comp")),
        check_vma=False,
    )
```

```python
import functools

import jax
import jax.numpy as jnp
from jax import lax
from jax.experimental import pallas as pl
from jax.experimental.pallas import tpu as pltpu
from jax.sharding import PartitionSpec as P

F32 = jnp.float32
VMEM_ALL = 63 << 20
LEV, ROWS, COLS = 16, 16, 1024
OLEV, OROWS, OCOLS = 10, 8, 512
WIDE = COLS + 128
OWIDE = OCOLS + 128
ANY = pl.BlockSpec(memory_space=pl.ANY)
SMEM = pl.BlockSpec(memory_space=pltpu.SMEM)


def lanes():
    return lax.broadcasted_iota(jnp.int32, (8, 128), 1)


def sublanes():
    return lax.broadcasted_iota(jnp.int32, (8, 128), 0)


def sweep(src, level, up_l, dn_l, rts, lts, wrap, edge, store):
    lane, sub = lanes(), sublanes()
    c, east, west, down, up = {}, {}, {}, {}, {}
    every = range(3) if wrap else rts
    nl = 9 if wrap else 8
    nr = len(every)

    def need(lt):
        if (0, every[0], lt) in c:
            return
        for f in range(3):
            for rt in every:
                v = src[f, level, rt * 8 : rt * 8 + 8, lt * 128 : lt * 128 + 128]
                c[f, rt, lt] = v
                if rt in rts:
                    east[f, rt, lt] = pltpu.roll(v, 1, 1)
                    west[f, rt, lt] = pltpu.roll(v, 127, 1)
                up[f, rt, lt] = pltpu.roll(v, 1, 0)
                down[f, rt, lt] = pltpu.roll(v, 7, 0)

    if wrap:
        need(8)
    need(0)
    for lt in lts:
        if wrap or lt < nl - 1:
            need((lt + 1) % nl)
        for rt in rts:
            inner = {
                "left": wrap or lt > 0,
                "right": wrap or lt < nl - 1,
                "prev": wrap or rt > 0,
                "next": wrap or rt < nr - 1,
            }
            out = {k: None if v else edge(k, rt, lt) for k, v in inner.items()}
            left, right, prev, nxt, four = {}, {}, {}, {}, {}
            for f in range(3):
                o = {k: out[k][f] if out[k] is not None else None for k in out}
                if inner["left"]:
                    o["left"] = east[f, rt, (lt - 1) % nl]
                if inner["right"]:
                    o["right"] = west[f, rt, (lt + 1) % nl]
                if inner["prev"]:
                    o["prev"] = up[f, (rt - 1) % nr, lt]
                if inner["next"]:
                    o["next"] = down[f, (rt + 1) % nr, lt]
                left[f] = jnp.where(lane == 0, o["left"], east[f, rt, lt])
                right[f] = jnp.where(lane == 127, o["right"], west[f, rt, lt])
                prev[f] = jnp.where(sub == 0, o["prev"], up[f, rt, lt])
                nxt[f] = jnp.where(sub == 7, o["next"], down[f, rt, lt])
                rows, cols = slice(rt * 8, rt * 8 + 8), slice(lt * 128, lt * 128 + 128)
                vert = src[f, up_l, rows, cols] + src[f, dn_l, rows, cols]
                four[f] = 2.0 * ((left[f] + right[f]) + (prev[f] + nxt[f])) + vert
            e = 0.06 * c[1, rt, lt] + 0.1 * (four[0] + (left[2] - right[2]))
            n = 0.1 * (four[1] + (prev[2] - nxt[2])) - 0.06 * c[0, rt, lt]
            h = 0.1 * (four[2] + (left[0] - right[0]) + (prev[1] - nxt[1]))
            store(rt, lt, (e, n, h))


def sideways(v, sign):
    e, n, h = v
    return (0.1 * (2.0 * e + sign * h), 0.2 * n, 0.1 * (2.0 * h + sign * e))


def upright(v, sign):
    e, n, h = v
    return (0.2 * e, 0.1 * (2.0 * n + sign * h), 0.1 * (2.0 * h + sign * n))


def neighbours():
    tile = lax.axis_index("tile")
    return tile > 0, tile < lax.axis_size("tile") - 1


def share(early):
    place = lax.axis_index("tile") % 16
    cut = jnp.where(place == 0, LEV // 2, 0)
    return (0, cut) if early else (cut, LEV)


def own_work(x, s1, s2, out_x, rb, cb, sem, ready, lo, hi):
    comp = lax.axis_index("comp")
    has_above, has_below = neighbours()
    zero = jnp.zeros((8, 128), F32)

    def first(level, _):
        ready(level)

        def store(rt, lt, new):
            for f in range(3):
                s1[f, level, rt * 8 : rt * 8 + 8, lt * 128 : lt * 128 + 128] = new[f]

        dn = jnp.minimum(level + 1, LEV - 1)
        sweep(x, level, jnp.maximum(level - 1, 0), dn, (0, 1), range(8), False, lambda *a: (zero,) * 3, store)
        return 0

    lax.fori_loop(jnp.maximum(lo - 1, 0), jnp.minimum(hi + 1, LEV), first, 0)
    gain = {
        "left": comp.astype(F32),
        "right": (1 - comp).astype(F32),
        "prev": has_above.astype(F32),
        "next": has_below.astype(F32),
    }

    def out_copy(level):
        return pltpu.make_async_copy(s2.at[:, level], out_x.at[:, level], sem)

    def second(level, _):
        def edge(kind, rt, lt):
            v = [x[f, level, rt * 8 : rt * 8 + 8, lt * 128 : lt * 128 + 128] for f in range(3)]
            put = sideways if kind in ("left", "right") else upright
            return [gain[kind] * w for w in put(v, -1.0 if kind in ("left", "prev") else 1.0)]

        def store(rt, lt, new):
            for f in range(3):
                s2[f, level, rt * 8 : rt * 8 + 8, lt * 128 : lt * 128 + 128] = new[f]

        dn = jnp.minimum(level + 1, LEV - 1)
        sweep(s1, level, jnp.maximum(level - 1, 0), dn, (0, 1), range(8), False, edge, store)
        out_copy(level).start()
        return 0

    lax.fori_loop(lo, hi, second, 0)
    es = pl.multiple_of((1 - comp) * (COLS - 128), 128)

    def kept(half):
        some = pl.ds(half * 8, 8)
        out = [pltpu.make_async_copy(s2.at[:, some, :, pl.ds(es, 128)], cb.at[:, some], sem)]
        for k, r in enumerate((0, 1, 15, 14)):
            for f in range(3):
                to = rb.at[pl.ds((k * 3 + f) * 16 + half * 8, 8), :]
                out.append(pltpu.make_async_copy(s2.at[f, some, r, :], to, sem))
        return out

    for half in range(2):

        @pl.when((lo <= half * 8) & (half * 8 < hi))
        def _():
            for c in kept(half):
                c.start()

    for half in range(2):

        @pl.when((lo <= half * 8) & (half * 8 < hi))
        def _():
            for c in kept(half):
                c.wait()

    lax.fori_loop(lo, hi, lambda l, _: (out_copy(l).wait(), 0)[1], 0)


def pack_kernel(
    x_in, ex_in, air_in, flow_in, warm_in,
    pay_up, pay_dn, swp,
    x, ex, air, flow, warm, packed, sems,
):
    comp = lax.axis_index("comp")
    cs = pl.multiple_of((1 - comp) * (COLS - 128), 128)
    os_ = pl.multiple_of((1 - comp) * (OCOLS - 128), 128)
    halves = [
        pltpu.make_async_copy(x_in.at[:, :, pl.ds(rt * 8, 8)], x.at[:, :, pl.ds(rt * 8, 8)], sems.at[2 + rt])
        for rt in range(2)
    ]
    loads = [
        pltpu.make_async_copy(a, b, sems.at[1])
        for a, b in ((ex_in, ex), (air_in, air), (flow_in, flow), (warm_in, warm))
    ]
    for c in halves[::-1] + loads:
        c.start()

    def rows_to(pay, rows):
        out = []
        for d in range(2):
            for f in range(3):
                out.append((x.at[f, :, rows[d], :], pay.at[pl.ds((d * 3 + f) * 16, 16), :]))
        for f in range(3):
            out.append((x.at[f, 0, rows[2], :], pay.at[104 + f, :]))
        return [pltpu.make_async_copy(a, b, sems.at[0]) for a, b in out]

    def surface_to(pay, edge, oedge):
        out = [(ex.at[edge, :], pay.at[107, :]), (air.at[edge, :], pay.at[108, :])]
        for k in range(2):
            cols = pl.ds(k * OCOLS, OCOLS)
            out.append((flow.at[k, pl.ds(0, 8), oedge, :], pay.at[pl.ds(96, 8), cols]))
            for lv in (8, 9):
                out.append((flow.at[k, lv, oedge, :], pay.at[101 + lv, cols]))
        out.append((warm.at[oedge, :], pay.at[111, pl.ds(0, OCOLS)]))
        return [pltpu.make_async_copy(a, b, sems.at[0]) for a, b in out]

    lane = lanes()
    back = 1 - comp
    sends = []

    def send(some):
        for c in some:
            c.start()
        sends.extend(some)

    for rt, pay, edges in ((1, pay_up, (15, 14, 13)), (0, pay_dn, (0, 1, 2))):
        halves[rt].wait()
        send(rows_to(pay, edges))
        acc = jnp.zeros((8, 128), F32)
        for g in range(48):
            v = x[g // 16, g % 16, rt * 8 : rt * 8 + 8, pl.ds(cs, 128)]
            v = pltpu.roll(v, (2 * g + 2 * back) % 128, 1)
            acc = jnp.where(lane // 2 == g, v, acc)
        packed[rt * 8 : rt * 8 + 8, :] = acc
        send(
            [
                pltpu.make_async_copy(
                    packed.at[pl.ds(rt * 8, 8), :], pay.at[pl.ds(112, 8), pl.ds(0, 128)], sems.at[0]
                )
            ]
        )
    for c in loads:
        c.wait()
    send(surface_to(pay_up, 15, 7) + surface_to(pay_dn, 0, 0))
    acc = jnp.zeros((8, 128), F32)
    for g in range(21):
        v = flow[g // 10, g % 10, :, pl.ds(os_, 128)] if g < 20 else warm[:, pl.ds(os_, 128)]
        v = pltpu.roll(v, g + back, 1)
        acc = jnp.where(lane == g, v, acc)
    packed[16:24, :] = acc
    swp[0:24, :] = packed[...]
    swp[24:32, :] = jnp.zeros((8, 128), F32)
    for c in sends:
        c.wait()


KEPT = ((3, LEV, ROWS, COLS), (192, COLS), (3, LEV, ROWS, 128))
STATE = pltpu.VMEM((3, LEV, ROWS, COLS), F32)


def pack(x, ex, air, flow, warm):
    vm = pl.BlockSpec(memory_space=pltpu.VMEM)
    sds = jax.ShapeDtypeStruct
    return pl.pallas_call(
        pack_kernel,
        out_shape=(
            sds((128, COLS), F32),
            sds((120, COLS), F32),
            sds((32, 128), F32),
        ),
        in_specs=[ANY] * 5,
        out_specs=(ANY, ANY, vm),
        scratch_shapes=[
            STATE,
            pltpu.VMEM((ROWS, COLS), F32),
            pltpu.VMEM((ROWS, COLS), F32),
            pltpu.VMEM((2, OLEV, OROWS, OCOLS), F32),
            pltpu.VMEM((OROWS, OCOLS), F32),
            pltpu.VMEM((24, 128), F32),
            pltpu.SemaphoreType.DMA((4,)),
        ],
        compiler_params=pltpu.CompilerParams(vmem_limit_bytes=VMEM_ALL),
        name="pack",
    )(x, ex, air, flow, warm)


def own_kernel(early, passed, x_in, *refs):
    out_x, rb, cb = refs[passed : passed + 3]
    x, s1, s2, sem, xsem = refs[-5:]
    lo, hi = share(early)

    @pl.when(lo < hi)
    def _():
        def load(level):
            return pltpu.make_async_copy(x_in.at[:, level], x.at[:, level], xsem.at[level])

        begin = jnp.maximum(lo - 2, 0)
        lax.fori_loop(begin, jnp.minimum(hi + 2, LEV), lambda l, _: (load(l).start(), 0)[1], 0)
        lax.fori_loop(begin, jnp.maximum(lo, 1), lambda l, _: (load(l).wait(), 0)[1], 0)

        def ready(level):
            @pl.when(level < LEV - 1)
            def _():
                load(level + 1).wait()

        own_work(x, s1, s2, out_x, rb, cb, sem, ready, lo, hi)


def own(x, early, passed):
    shapes = [v.shape for v in passed] if not early else [v.shape for v in passed] + list(KEPT)
    aliased = {i + 1: i for i in range(len(passed))}
    return pl.pallas_call(
        functools.partial(own_kernel, early, len(shapes) + len(passed) - 3),
        out_shape=tuple(jax.ShapeDtypeStruct(k, F32) for k in shapes),
        in_specs=[ANY] * (1 + len(passed)),
        out_specs=(ANY,) * len(shapes),
        input_output_aliases=aliased,
        scratch_shapes=[STATE, STATE, STATE, pltpu.SemaphoreType.DMA, pltpu.SemaphoreType.DMA((LEV,))],
        compiler_params=pltpu.CompilerParams(vmem_limit_bytes=VMEM_ALL),
        name="own_early" if early else "own_late",
    )(x, *passed)


def row_terms(near, far, mid, edge, kept, sign):
    lane, sub = lanes(), sublanes()
    zero = jnp.zeros((8, 128), F32)

    def at(ref, f, st, lt):
        return ref[f * 16 + st * 8 : f * 16 + st * 8 + 8, lt * 128 : lt * 128 + 128]

    def full(src, out, put):
        for lt in range(8):
            for st in range(2):
                c, left, right, four = {}, {}, {}, {}
                o = [at(out, f, st, lt) for f in range(3)]
                for f in range(3):
                    c[f] = at(src, f, st, lt)
                    lo = pltpu.roll(at(src, f, st, lt - 1), 1, 1) if lt > 0 else zero
                    hi = pltpu.roll(at(src, f, st, lt + 1), 127, 1) if lt < 7 else zero
                    left[f] = jnp.where(lane == 0, lo, pltpu.roll(c[f], 1, 1))
                    right[f] = jnp.where(lane == 127, hi, pltpu.roll(c[f], 127, 1))
                    other = at(src, f, 1 - st, lt)
                    above = jnp.where(sub == 0, c[f] if st == 0 else pltpu.roll(other, 1, 0), pltpu.roll(c[f], 1, 0))
                    below = jnp.where(sub == 7, c[f] if st == 1 else pltpu.roll(other, 7, 0), pltpu.roll(c[f], 7, 0))
                    four[f] = 2.0 * (left[f] + right[f] + o[f]) + (above + below)
                e = 0.06 * c[1] + 0.1 * (four[0] + (left[2] - right[2]))
                n = 0.1 * (four[1] + sign * o[2]) - 0.06 * c[0]
                h = 0.1 * (four[2] + (left[0] - right[0]) + sign * o[1])
                put(st, lt, (e, n, h))

    def put_edge(st, lt, new):
        for f in range(3):
            edge[f * 16 + st * 8 : f * 16 + st * 8 + 8, lt * 128 : lt * 128 + 128] = new[f]

    full(near, far, put_edge)
    for lt in range(8):
        for st in range(2):
            y = upright([at(near, f, st, lt) for f in range(3)], sign)
            z = upright(y, sign)
            for f in range(3):
                rows, cols = slice(f * 16 + st * 8, f * 16 + st * 8 + 8), slice(lt * 128, lt * 128 + 128)
                mid[rows, cols] = y[f]
                kept[48 + f * 16 + st * 8 : 48 + f * 16 + st * 8 + 8, cols] += z[f]

    def put_kept(st, lt, new):
        for f in range(3):
            kept[f * 16 + st * 8 : f * 16 + st * 8 + 8, lt * 128 : lt * 128 + 128] += new[f]

    full(mid, edge, put_kept)


def column_terms(tiles, comp):
    lane, sub = lanes(), sublanes()
    flip = jnp.where(comp == 1, 1.0, -1.0)
    right_half = comp == 1
    x1, x2 = [[], [], []], [[], [], []]
    for v in tiles:
        w = pltpu.roll(v, 127, 1)
        a = jnp.where(right_half, w, v)
        b = jnp.where(right_half, v, w)
        for f in range(3):
            x1[f].append(pltpu.roll(a, (128 - 32 * f) % 128, 1))
            x2[f].append(pltpu.roll(b, (128 - 32 * f) % 128, 1))

    def lateral(v):
        per_tile = [sideways([v[f][k] for f in range(3)], flip) for k in range(len(v[0]))]
        return [[p[f] for p in per_tile] for f in range(3)]

    def full(c, out):
        res = [[], [], []]
        for rt in range(2):
            prev, nxt, four = {}, {}, {}
            for f in range(3):
                v = c[f][rt]
                p = c[f][2] if rt == 0 else c[f][0]
                q = c[f][1] if rt == 0 else c[f][2]
                prev[f] = jnp.where(sub == 0, pltpu.roll(p, 1, 0), pltpu.roll(v, 1, 0))
                nxt[f] = jnp.where(sub == 7, pltpu.roll(q, 7, 0), pltpu.roll(v, 7, 0))
                above = jnp.where(lane < 2, v, pltpu.roll(v, 2, 1))
                below = jnp.where(lane >= 30, v, pltpu.roll(v, 126, 1))
                four[f] = 2.0 * (prev[f] + nxt[f] + out[f][rt]) + (above + below)
            res[0].append(0.06 * c[1][rt] + 0.1 * (four[0] + flip * out[2][rt]))
            res[1].append(0.1 * (four[1] + (prev[2] - nxt[2])) - 0.06 * c[0][rt])
            res[2].append(0.1 * (four[2] + flip * out[0][rt] + (prev[1] - nxt[1])))
        return res

    y = lateral(x1)
    s0 = full(y, full(x1, x2))
    s1 = lateral([[v[0], v[1]] for v in y])
    pairs = []
    for f in range(3):
        row = []
        for rt in range(2):
            a = jnp.where(right_half, s0[f][rt], s1[f][rt])
            b = jnp.where(right_half, s1[f][rt], s0[f][rt])
            row.append(jnp.where(lane % 2 == 0, a, pltpu.roll(b, 1, 1)))
        pairs.append(row)
    return pairs


def rows_kernel(pay_up, pay_dn, x_own, rb, out_x, ke, halo_rows, mid, edge, kept, sems):
    comp = lax.axis_index("comp")
    loads = [
        pltpu.make_async_copy(rb, kept, sems.at[0]),
        pltpu.make_async_copy(pay_up.at[pl.ds(0, 96), :], halo_rows.at[0], sems.at[0]),
        pltpu.make_async_copy(pay_dn.at[pl.ds(0, 96), :], halo_rows.at[1], sems.at[0]),
    ]
    for c in loads:
        c.start()
    for c in loads:
        c.wait()
    rest = pl.multiple_of(comp * 128, 128)
    es = pl.multiple_of((1 - comp) * (COLS - 128), 128)
    puts = [
        pltpu.make_async_copy(
            kept.at[pl.ds((k * 3 + f) * 16, 16), pl.ds(rest, COLS - 128)],
            out_x.at[f, :, r, pl.ds(rest, COLS - 128)],
            sems.at[1],
        )
        for k, r in enumerate((0, 1, 15, 14))
        for f in range(3)
    ]
    for side, there in enumerate(neighbours()):

        @pl.when(there)
        def _():
            rows = halo_rows.at[side]
            row_terms(
                rows.at[pl.ds(0, 48)], rows.at[pl.ds(48, 48)], mid, edge,
                kept.at[pl.ds(side * 96, 96)], 1.0 if side == 0 else -1.0,
            )

        for c in puts[side * 6 : side * 6 + 6]:
            c.start()
    puts.append(pltpu.make_async_copy(kept.at[:, pl.ds(es, 128)], ke, sems.at[1]))
    puts[-1].start()
    for c in puts:
        c.wait()


def rows(pay_up, pay_dn, x_own, rb):
    sds = jax.ShapeDtypeStruct
    return pl.pallas_call(
        rows_kernel,
        out_shape=(sds(x_own.shape, F32), sds((192, 128), F32)),
        in_specs=[ANY] * 4,
        out_specs=(ANY, ANY),
        input_output_aliases={2: 0},
        scratch_shapes=[
            pltpu.VMEM((2, 96, COLS), F32),
            pltpu.VMEM((48, COLS), F32),
            pltpu.VMEM((48, COLS), F32),
            pltpu.VMEM((192, COLS), F32),
            pltpu.SemaphoreType.DMA((2,)),
        ],
        compiler_params=pltpu.CompilerParams(vmem_limit_bytes=VMEM_ALL),
        name="rows",
    )(pay_up, pay_dn, x_own, rb)


def final_kernel(
    x, ex, air, flow, warm, water, part, tally, wgt, pay_up, pay_dn, swp, x_own, ke, cb,
    out_x, out_flow, out_warm,
    s0, s1, kept, cbv, cbo, coef, blocks, wv, res, oc, mask, of, ow, small, sems,
):
    comp = lax.axis_index("comp")
    tile = lax.axis_index("tile")
    lane, sub = lanes(), sublanes()
    has_above, has_below = neighbours()

    def halo(pay, rows, third):
        out = []
        for d in range(2):
            for f in range(3):
                for lv in range(3 - d):
                    out.append((pay.at[(d * 3 + f) * 16 + lv, :], s0.at[f, lv, rows[d], pl.ds(0, COLS)]))
        for f in range(3):
            out.append((pay.at[104 + f, :], s0.at[f, 0, rows[2], pl.ds(0, COLS)]))
        to = pl.ds(0, OCOLS)
        for k in range(2):
            out.append((pay.at[107 + k, :], coef.at[k, rows[0], :]))
            cols = pl.ds(k * OCOLS, OCOLS)
            out.append((pay.at[pl.ds(96, 8), cols], oc.at[pl.ds(k * 10, 8), third, to]))
            for lv in (8, 9):
                out.append((pay.at[101 + lv, cols], oc.at[k * 10 + lv, third, to]))
        out.append((pay.at[111, to], oc.at[20, third, to]))
        return [pltpu.make_async_copy(a, b, sems.at[1]) for a, b in out]

    above = ((23, 22, 21), 8)
    below = ((16, 17, 18), 15)
    keeps = [pltpu.make_async_copy(ke, kept, sems.at[2]), pltpu.make_async_copy(cb, cbv, sems.at[2])]
    smalls = [pltpu.make_async_copy(swp, small, sems.at[3])]
    mine = [
        pltpu.make_async_copy(x.at[:, pl.ds(0, 3)], s0.at[:, :, pl.ds(0, 16), pl.ds(0, COLS)], sems.at[4]),
        pltpu.make_async_copy(ex, coef.at[0, pl.ds(0, 16), :], sems.at[4]),
        pltpu.make_async_copy(air, coef.at[1, pl.ds(0, 16), :], sems.at[4]),
        pltpu.make_async_copy(flow.at[0], oc.at[pl.ds(0, 10), pl.ds(0, 8), pl.ds(0, OCOLS)], sems.at[4]),
        pltpu.make_async_copy(flow.at[1], oc.at[pl.ds(10, 10), pl.ds(0, 8), pl.ds(0, OCOLS)], sems.at[4]),
        pltpu.make_async_copy(warm, oc.at[20, pl.ds(0, 8), pl.ds(0, OCOLS)], sems.at[4]),
        pltpu.make_async_copy(water, mask, sems.at[4]),
    ]
    wcopy = pltpu.make_async_copy(wgt, wv, sems.at[5])

    halos = halo(pay_up, *above) + halo(pay_dn, *below)
    for c in halos:
        c.start()
    for c in smalls + mine + keeps + [wcopy]:
        c.start()
    for c in smalls:
        c.wait()

    row_ok = jnp.where(sub >= 4, has_above.astype(jnp.int32), has_below.astype(jnp.int32)) > 0
    row_halo = jnp.where(sub < 4, has_above.astype(jnp.int32), has_below.astype(jnp.int32)) > 0
    edge2 = jnp.where(comp == 0, lane, 127 - lane) < 2
    edge1 = jnp.where(comp == 0, lane, 127 - lane) < 1
    corner = jnp.where(row_ok, small[24:32, :], 0.0)
    for f in range(3):
        for lv in range(3):
            shift = (128 - 2 * (f * 16 + lv) + 126 * comp) % 128
            for rt in range(3):
                v = small[rt * 8 : rt * 8 + 8, :] if rt < 2 else corner
                s0[f, lv, rt * 8 : rt * 8 + 8, COLS:WIDE] = jnp.where(edge2, pltpu.roll(v, shift, 1), 0.0)

    for c in mine:
        c.wait()
    for c in halos:
        c.wait()

    @pl.when(jnp.logical_not(has_above & has_below))
    def _():
        for lt in range(8):
            cols = slice(lt * 128, lt * 128 + 128)
            for f in range(3):
                for lv in range(3):
                    s0[f, lv, 16:24, cols] = jnp.where(row_ok, s0[f, lv, 16:24, cols], 0.0)

        def oclear(g, _):
            for lt in range(4):
                cols = slice(lt * 128, lt * 128 + 128)
                oc[g, 8:16, cols] = jnp.where(row_halo, oc[g, 8:16, cols], 0.0)
            return 0

        lax.fori_loop(0, 21, oclear, 0)

    for level in range(2):

        def put_first(rt, lt, new):
            rows, cols = slice(rt * 8, rt * 8 + 8), slice(lt * 128, lt * 128 + 128)
            for f in range(3):
                v = new[f]
                if lt == 8:
                    v = jnp.where(edge1 & row_ok if rt == 2 else edge1, v, 0.0)
                elif rt == 2:
                    v = jnp.where(row_ok, v, 0.0)
                s1[f, level, rows, cols] = v

        sweep(s0, level, 0, level + 1, range(3), range(9), True, None, put_first)

    def put_flux(rt, lt, new):
        rows, cols = slice(rt * 8, rt * 8 + 8), slice(lt * 128, lt * 128 + 128)
        e, n, h = new
        mult = coef[0, rows, cols] * jnp.sqrt(e * e + n * n + 0.25)
        at = rt * 512 + lt * 8
        for f, v in enumerate((mult * e, mult * n, mult * (coef[1, rows, cols] - h))):
            hi = v.astype(jnp.bfloat16).astype(F32)
            blocks[pl.ds(at + f, 8, stride=64), :] = hi
            blocks[pl.ds(at + 3 + f, 8, stride=64), :] = v - hi
        blocks[pl.ds(at + 6, 8, stride=64), :] = jnp.ones((8, 128), F32)
        blocks[pl.ds(at + 7, 8, stride=64), :] = jnp.zeros((8, 128), F32)

    sweep(s1, 0, 0, 1, range(3), range(8), True, None, put_flux)

    for c in keeps:
        c.wait()
    es = pl.multiple_of((1 - comp) * (COLS - 128), 128)
    pairs = column_terms((small[0:8, :], small[8:16, :], corner), comp)
    own2 = jnp.where(comp == 0, 127 - lane, lane) < 2
    for f in range(3):
        for lv in range(16):
            shift = (128 - 2 * lv + 126 * (1 - comp)) % 128
            for rt in range(2):
                v = cbv[f, lv, rt * 8 : rt * 8 + 8, :]
                for k, at in ((0, 0), (1, 1)) if rt == 0 else ((2, 7), (3, 6)):
                    line = kept[(k * 3 + f) * 16 + lv : (k * 3 + f) * 16 + lv + 1, :]
                    v = jnp.where(sub == at, line, v)
                v = v + jnp.where(own2, pltpu.roll(pairs[f][rt], shift, 1), 0.0)
                cbo[f, lv, rt * 8 : rt * 8 + 8, :] = v
    put_edge = pltpu.make_async_copy(cbo, out_x.at[:, :, :, pl.ds(es, 128)], sems.at[7])
    put_edge.start()

    wcopy.wait()
    base = tile * 128

    def remap(g, _):
        live = tally[g]
        parts = []
        for s in range(4):
            p = part[s, g] - base
            p = jnp.where(p < 0, p + 192, p)
            row = pl.multiple_of(p * 8, 8)
            v = blocks[pl.ds(row, 8), :]
            parts.append(v * jnp.where(s < live, 1.0, 0.0))
        lhs = jnp.concatenate(parts, axis=1).astype(jnp.bfloat16)
        rhs = wv[g].reshape(512, 128)
        res[pl.ds(pl.multiple_of(g * 8, 8), 8), :] = jnp.dot(lhs, rhs, preferred_element_type=F32)
        return 0

    lax.fori_loop(0, 32, remap, 0, unroll=32)

    def unpack_ocean():
        for g in range(21):
            shift = (128 - g + 127 * comp) % 128
            v = pltpu.roll(small[16:24, :], shift, 1)
            oc[g, 0:8, OCOLS:OWIDE] = jnp.where(edge1, v, 0.0)

    unpack_ocean()

    def around(g, lt):
        cols = slice(lt * 128, lt * 128 + 128)
        c = oc[g, 0:8, cols]
        hv = oc[g, 8:16, cols]
        lo, hi = (lt - 1) % 5, lt + 1
        left = jnp.where(lane == 0, pltpu.roll(oc[g, 0:8, lo * 128 : lo * 128 + 128], 1, 1), pltpu.roll(c, 1, 1))
        right = jnp.where(lane == 127, pltpu.roll(oc[g, 0:8, hi * 128 : hi * 128 + 128], 127, 1), pltpu.roll(c, 127, 1))
        prev = jnp.where(sub == 0, hv, pltpu.roll(c, 1, 0))
        nxt = jnp.where(sub == 7, hv, pltpu.roll(c, 7, 0))
        return c, left, right, prev, nxt

    for lt in range(4):
        cols = slice(lt * 128, lt * 128 + 128)
        m = mask[:, cols].astype(F32)
        den = res[pl.ds(lt * 8 + 6, 8, stride=32), :]
        rem = [
            (res[pl.ds(lt * 8 + f, 8, stride=32), :] + res[pl.ds(lt * 8 + f + 3, 8, stride=32), :]) / den
            for f in range(3)
        ]
        for k in range(2):
            for lv in range(10):
                g = k * 10 + lv
                c, left, right, prev, nxt = around(g, lt)
                other = oc[(1 - k) * 10 + lv, 0:8, cols]
                vert = oc[k * 10 + max(lv - 1, 0), 0:8, cols] + oc[k * 10 + min(lv + 1, 9), 0:8, cols]
                v = 0.2 * ((left + right) + (prev + nxt)) + 0.1 * vert
                v = v + (0.06 if k == 0 else -0.06) * other
                if lv == 0:
                    v = v + 0.2 * rem[k]
                of[k, lv, :, cols] = m * v
        c, left, right, prev, nxt = around(20, lt)
        lap = (left + right) + (prev + nxt) - 4.0 * c
        carried = oc[0, 0:8, cols] * (0.5 * (right - left)) + oc[10, 0:8, cols] * (0.5 * (nxt - prev))
        ow[:, cols] = c + (m * 0.2) * (rem[2] - carried + 0.5 * lap)
    tail = [
        pltpu.make_async_copy(of, out_flow, sems.at[8]),
        pltpu.make_async_copy(ow, out_warm, sems.at[8]),
    ]
    for c in tail:
        c.start()
    for c in tail + [put_edge]:
        c.wait()


def final(x, ex, air, flow, warm, water, part, tally, wgt, halos, kept):
    sds = jax.ShapeDtypeStruct
    return pl.pallas_call(
        final_kernel,
        out_shape=(sds(x.shape, F32), sds(flow.shape, F32), sds(warm.shape, F32)),
        in_specs=[ANY] * 6 + [SMEM] * 2 + [ANY] * 7,
        out_specs=(ANY, ANY, ANY),
        input_output_aliases={12: 0},
        scratch_shapes=[
            pltpu.VMEM((3, 3, 24, WIDE), F32),
            pltpu.VMEM((3, 2, 24, WIDE), F32),
            pltpu.VMEM((192, 128), F32),
            pltpu.VMEM((3, LEV, ROWS, 128), F32),
            pltpu.VMEM((3, LEV, ROWS, 128), F32),
            pltpu.VMEM((2, 24, COLS), F32),
            pltpu.VMEM((24 * 64, 128), F32),
            pltpu.VMEM((32, 4, 128, 128), jnp.bfloat16),
            pltpu.VMEM((256, 128), F32),
            pltpu.VMEM((21, 16, OWIDE), F32),
            pltpu.VMEM((OROWS, OCOLS), jnp.int32),
            pltpu.VMEM((2, OLEV, OROWS, OCOLS), F32),
            pltpu.VMEM((OROWS, OCOLS), F32),
            pltpu.VMEM((32, 128), F32),
            pltpu.SemaphoreType.DMA((9,)),
        ],
        compiler_params=pltpu.CompilerParams(vmem_limit_bytes=VMEM_ALL),
        name="final",
    )(x, ex, air, flow, warm, water, part, tally, wgt, *halos, *kept)


def shift(v, step, across):
    tiles = lax.axis_size("tile")
    if not across:
        return lax.ppermute(v, "tile", [(t, (t + step) % tiles) for t in range(tiles)])
    perm = [(c * tiles + t, (1 - c) * tiles + (t + step) % tiles) for c in range(2) for t in range(tiles)]
    return lax.ppermute(v, ("comp", "tile"), perm)


def shards(x, ex, air, flow, warm, water, part, tally, wgt):
    pay_up, pay_dn, swp = pack(x, ex, air, flow, warm)
    got_up = shift(pay_up, 1, False)
    pay_dn, *kept = own(x, True, [pay_dn])
    got_dn = shift(pay_dn, -1, False)
    swp, x_own, rb, cb = own(x, False, [swp, *kept])
    upper = lax.broadcasted_iota(jnp.int32, (8, 128), 0) >= 4
    corner = jnp.where(upper, got_up[112:120, :128], got_dn[112:120, :128])
    got_sw = shift(lax.dynamic_update_slice(swp, corner, (24, 0)), 0, True)
    x_own, ke = rows(got_up, got_dn, x_own, rb)
    return final(x, ex, air, flow, warm, water, part.T, tally, wgt, (got_up, got_dn, got_sw), (x_own, ke, cb))


def solution(mesh):
    placed = (
        P(None, None, "tile", "comp"),
        P("tile", "comp"),
        P("tile", "comp"),
        P(None, None, "tile", "comp"),
        P("tile", "comp"),
        P("tile", "comp"),
        P(("comp", "tile"), None),
        P(("comp", "tile")),
        P(("comp", "tile"), None, None, None),
    )
    return jax.shard_map(
        shards,
        mesh=mesh,
        in_specs=placed,
        out_specs=(P(None, None, "tile", "comp"), P(None, None, "tile", "comp"), P("tile", "comp")),
        check_vma=False,
    )
```

```python
import functools

import jax
import jax.numpy as jnp
from jax import lax
from jax.experimental import pallas as pl
from jax.experimental.pallas import tpu as pltpu
from jax.sharding import PartitionSpec as P

F32 = jnp.float32
VMEM_ALL = 63 << 20
LEV, ROWS, COLS = 16, 16, 1024
OLEV, OROWS, OCOLS = 10, 8, 512
WIDE = COLS + 128
OWIDE = OCOLS + 128
ANY = pl.BlockSpec(memory_space=pl.ANY)
SMEM = pl.BlockSpec(memory_space=pltpu.SMEM)


def lanes():
    return lax.broadcasted_iota(jnp.int32, (8, 128), 1)


def sublanes():
    return lax.broadcasted_iota(jnp.int32, (8, 128), 0)


def sweep(src, level, up_l, dn_l, rts, lts, wrap, edge, store):
    lane, sub = lanes(), sublanes()
    c, east, west, down, up = {}, {}, {}, {}, {}
    every = range(3) if wrap else rts
    nl = 9 if wrap else 8
    nr = len(every)

    def need(lt):
        if (0, every[0], lt) in c:
            return
        for f in range(3):
            for rt in every:
                v = src[f, level, rt * 8 : rt * 8 + 8, lt * 128 : lt * 128 + 128]
                c[f, rt, lt] = v
                if rt in rts:
                    east[f, rt, lt] = pltpu.roll(v, 1, 1)
                    west[f, rt, lt] = pltpu.roll(v, 127, 1)
                up[f, rt, lt] = pltpu.roll(v, 1, 0)
                down[f, rt, lt] = pltpu.roll(v, 7, 0)

    if wrap:
        need(8)
    need(0)
    for lt in lts:
        if wrap or lt < nl - 1:
            need((lt + 1) % nl)
        for rt in rts:
            inner = {
                "left": wrap or lt > 0,
                "right": wrap or lt < nl - 1,
                "prev": wrap or rt > 0,
                "next": wrap or rt < nr - 1,
            }
            out = {k: None if v else edge(k, rt, lt) for k, v in inner.items()}
            left, right, prev, nxt, four = {}, {}, {}, {}, {}
            for f in range(3):
                o = {k: out[k][f] if out[k] is not None else None for k in out}
                if inner["left"]:
                    o["left"] = east[f, rt, (lt - 1) % nl]
                if inner["right"]:
                    o["right"] = west[f, rt, (lt + 1) % nl]
                if inner["prev"]:
                    o["prev"] = up[f, (rt - 1) % nr, lt]
                if inner["next"]:
                    o["next"] = down[f, (rt + 1) % nr, lt]
                left[f] = jnp.where(lane == 0, o["left"], east[f, rt, lt])
                right[f] = jnp.where(lane == 127, o["right"], west[f, rt, lt])
                prev[f] = jnp.where(sub == 0, o["prev"], up[f, rt, lt])
                nxt[f] = jnp.where(sub == 7, o["next"], down[f, rt, lt])
                rows, cols = slice(rt * 8, rt * 8 + 8), slice(lt * 128, lt * 128 + 128)
                vert = src[f, up_l, rows, cols] + src[f, dn_l, rows, cols]
                four[f] = 2.0 * ((left[f] + right[f]) + (prev[f] + nxt[f])) + vert
            e = 0.06 * c[1, rt, lt] + 0.1 * (four[0] + (left[2] - right[2]))
            n = 0.1 * (four[1] + (prev[2] - nxt[2])) - 0.06 * c[0, rt, lt]
            h = 0.1 * (four[2] + (left[0] - right[0]) + (prev[1] - nxt[1]))
            store(rt, lt, (e, n, h))


def sideways(v, sign):
    e, n, h = v
    return (0.1 * (2.0 * e + sign * h), 0.2 * n, 0.1 * (2.0 * h + sign * e))


def upright(v, sign):
    e, n, h = v
    return (0.2 * e, 0.1 * (2.0 * n + sign * h), 0.1 * (2.0 * h + sign * n))


def neighbours():
    tile = lax.axis_index("tile")
    return tile > 0, tile < lax.axis_size("tile") - 1


def share(early):
    place = lax.axis_index("tile") % 16
    cut = jnp.where(place == 0, LEV // 2, 0)
    return (0, cut) if early else (cut, LEV)


def own_work(x, s1, s2, out_x, rb, cb, sem, ready, lo, hi):
    comp = lax.axis_index("comp")
    has_above, has_below = neighbours()
    zero = jnp.zeros((8, 128), F32)

    def first(level, _):
        ready(level)

        def store(rt, lt, new):
            for f in range(3):
                s1[f, level, rt * 8 : rt * 8 + 8, lt * 128 : lt * 128 + 128] = new[f]

        dn = jnp.minimum(level + 1, LEV - 1)
        sweep(x, level, jnp.maximum(level - 1, 0), dn, (0, 1), range(8), False, lambda *a: (zero,) * 3, store)
        return 0

    lax.fori_loop(jnp.maximum(lo - 1, 0), jnp.minimum(hi + 1, LEV), first, 0)
    gain = {
        "left": comp.astype(F32),
        "right": (1 - comp).astype(F32),
        "prev": has_above.astype(F32),
        "next": has_below.astype(F32),
    }

    def out_copy(level):
        return pltpu.make_async_copy(s2.at[:, level], out_x.at[:, level], sem)

    def second(level, _):
        def edge(kind, rt, lt):
            v = [x[f, level, rt * 8 : rt * 8 + 8, lt * 128 : lt * 128 + 128] for f in range(3)]
            put = sideways if kind in ("left", "right") else upright
            return [gain[kind] * w for w in put(v, -1.0 if kind in ("left", "prev") else 1.0)]

        def store(rt, lt, new):
            for f in range(3):
                s2[f, level, rt * 8 : rt * 8 + 8, lt * 128 : lt * 128 + 128] = new[f]

        dn = jnp.minimum(level + 1, LEV - 1)
        sweep(s1, level, jnp.maximum(level - 1, 0), dn, (0, 1), range(8), False, edge, store)
        out_copy(level).start()
        return 0

    es = pl.multiple_of((1 - comp) * (COLS - 128), 128)

    def kept(half):
        some = pl.ds(half * 8, 8)
        out = [pltpu.make_async_copy(s2.at[:, some, :, pl.ds(es, 128)], cb.at[:, some], sem)]
        for k, r in enumerate((0, 1, 15, 14)):
            for f in range(3):
                to = rb.at[pl.ds((k * 3 + f) * 16 + half * 8, 8), :]
                out.append(pltpu.make_async_copy(s2.at[f, some, r, :], to, sem))
        return out

    for half in range(2):

        @pl.when((lo <= half * 8) & (half * 8 < hi))
        def _():
            lax.fori_loop(half * 8, half * 8 + 8, second, 0, unroll=2)
            for c in kept(half):
                c.start()

    for half in range(2):

        @pl.when((lo <= half * 8) & (half * 8 < hi))
        def _():
            for c in kept(half):
                c.wait()

    lax.fori_loop(lo, hi, lambda l, _: (out_copy(l).wait(), 0)[1], 0)


def pack_kernel(
    x_in, ex_in, air_in, flow_in, warm_in,
    pay_up, pay_dn, swp,
    x, ex, air, flow, warm, packed, sems,
):
    comp = lax.axis_index("comp")
    cs = pl.multiple_of((1 - comp) * (COLS - 128), 128)
    os_ = pl.multiple_of((1 - comp) * (OCOLS - 128), 128)
    halves = [
        pltpu.make_async_copy(x_in.at[:, :, pl.ds(rt * 8, 8)], x.at[:, :, pl.ds(rt * 8, 8)], sems.at[2 + rt])
        for rt in range(2)
    ]
    loads = [
        pltpu.make_async_copy(a, b, sems.at[1])
        for a, b in ((ex_in, ex), (air_in, air), (flow_in, flow), (warm_in, warm))
    ]
    for c in halves[::-1] + loads:
        c.start()

    def rows_to(pay, rows):
        out = []
        for d in range(2):
            for f in range(3):
                out.append((x.at[f, :, rows[d], :], pay.at[pl.ds((d * 3 + f) * 16, 16), :]))
        for f in range(3):
            out.append((x.at[f, 0, rows[2], :], pay.at[104 + f, :]))
        return [pltpu.make_async_copy(a, b, sems.at[0]) for a, b in out]

    def surface_to(pay, edge, oedge):
        out = [(ex.at[edge, :], pay.at[107, :]), (air.at[edge, :], pay.at[108, :])]
        for k in range(2):
            cols = pl.ds(k * OCOLS, OCOLS)
            out.append((flow.at[k, pl.ds(0, 8), oedge, :], pay.at[pl.ds(96, 8), cols]))
            for lv in (8, 9):
                out.append((flow.at[k, lv, oedge, :], pay.at[101 + lv, cols]))
        out.append((warm.at[oedge, :], pay.at[111, pl.ds(0, OCOLS)]))
        return [pltpu.make_async_copy(a, b, sems.at[0]) for a, b in out]

    lane = lanes()
    back = 1 - comp
    sends = []

    def send(some):
        for c in some:
            c.start()
        sends.extend(some)

    for rt, pay, edges in ((1, pay_up, (15, 14, 13)), (0, pay_dn, (0, 1, 2))):
        halves[rt].wait()
        send(rows_to(pay, edges))
        acc = jnp.zeros((8, 128), F32)
        for g in range(48):
            v = x[g // 16, g % 16, rt * 8 : rt * 8 + 8, pl.ds(cs, 128)]
            v = pltpu.roll(v, (2 * g + 2 * back) % 128, 1)
            acc = jnp.where(lane // 2 == g, v, acc)
        packed[rt * 8 : rt * 8 + 8, :] = acc
        send(
            [
                pltpu.make_async_copy(
                    packed.at[pl.ds(rt * 8, 8), :], pay.at[pl.ds(112, 8), pl.ds(0, 128)], sems.at[0]
                )
            ]
        )
    for c in loads:
        c.wait()
    send(surface_to(pay_up, 15, 7) + surface_to(pay_dn, 0, 0))
    acc = jnp.zeros((8, 128), F32)
    for g in range(21):
        v = flow[g // 10, g % 10, :, pl.ds(os_, 128)] if g < 20 else warm[:, pl.ds(os_, 128)]
        v = pltpu.roll(v, g + back, 1)
        acc = jnp.where(lane == g, v, acc)
    packed[16:24, :] = acc
    swp[0:24, :] = packed[...]
    swp[24:32, :] = jnp.zeros((8, 128), F32)
    for c in sends:
        c.wait()


KEPT = ((3, LEV, ROWS, COLS), (192, COLS), (3, LEV, ROWS, 128))
STATE = pltpu.VMEM((3, LEV, ROWS, COLS), F32)


def pack(x, ex, air, flow, warm):
    vm = pl.BlockSpec(memory_space=pltpu.VMEM)
    sds = jax.ShapeDtypeStruct
    return pl.pallas_call(
        pack_kernel,
        out_shape=(
            sds((128, COLS), F32),
            sds((120, COLS), F32),
            sds((32, 128), F32),
        ),
        in_specs=[ANY] * 5,
        out_specs=(ANY, ANY, vm),
        scratch_shapes=[
            STATE,
            pltpu.VMEM((ROWS, COLS), F32),
            pltpu.VMEM((ROWS, COLS), F32),
            pltpu.VMEM((2, OLEV, OROWS, OCOLS), F32),
            pltpu.VMEM((OROWS, OCOLS), F32),
            pltpu.VMEM((24, 128), F32),
            pltpu.SemaphoreType.DMA((4,)),
        ],
        compiler_params=pltpu.CompilerParams(vmem_limit_bytes=VMEM_ALL),
        name="pack",
    )(x, ex, air, flow, warm)


def own_kernel(early, passed, x_in, *refs):
    out_x, rb, cb = refs[passed : passed + 3]
    x, s1, s2, sem, xsem = refs[-5:]
    lo, hi = share(early)

    @pl.when(lo < hi)
    def _():
        def load(level):
            return pltpu.make_async_copy(x_in.at[:, level], x.at[:, level], xsem.at[level])

        begin = jnp.maximum(lo - 2, 0)
        lax.fori_loop(begin, jnp.minimum(hi + 2, LEV), lambda l, _: (load(l).start(), 0)[1], 0)
        lax.fori_loop(begin, jnp.maximum(lo, 1), lambda l, _: (load(l).wait(), 0)[1], 0)

        def ready(level):
            @pl.when(level < LEV - 1)
            def _():
                load(level + 1).wait()

        own_work(x, s1, s2, out_x, rb, cb, sem, ready, lo, hi)


def own(x, early, passed):
    shapes = [v.shape for v in passed] if not early else [v.shape for v in passed] + list(KEPT)
    aliased = {i + 1: i for i in range(len(passed))}
    return pl.pallas_call(
        functools.partial(own_kernel, early, len(shapes) + len(passed) - 3),
        out_shape=tuple(jax.ShapeDtypeStruct(k, F32) for k in shapes),
        in_specs=[ANY] * (1 + len(passed)),
        out_specs=(ANY,) * len(shapes),
        input_output_aliases=aliased,
        scratch_shapes=[STATE, STATE, STATE, pltpu.SemaphoreType.DMA, pltpu.SemaphoreType.DMA((LEV,))],
        compiler_params=pltpu.CompilerParams(vmem_limit_bytes=VMEM_ALL),
        name="own_early" if early else "own_late",
    )(x, *passed)


def row_terms(near, far, mid, edge, kept, sign):
    lane, sub = lanes(), sublanes()
    zero = jnp.zeros((8, 128), F32)

    def at(ref, f, st, lt):
        return ref[f * 16 + st * 8 : f * 16 + st * 8 + 8, lt * 128 : lt * 128 + 128]

    def full(src, out, put):
        for lt in range(8):
            for st in range(2):
                c, left, right, four = {}, {}, {}, {}
                o = [at(out, f, st, lt) for f in range(3)]
                for f in range(3):
                    c[f] = at(src, f, st, lt)
                    lo = pltpu.roll(at(src, f, st, lt - 1), 1, 1) if lt > 0 else zero
                    hi = pltpu.roll(at(src, f, st, lt + 1), 127, 1) if lt < 7 else zero
                    left[f] = jnp.where(lane == 0, lo, pltpu.roll(c[f], 1, 1))
                    right[f] = jnp.where(lane == 127, hi, pltpu.roll(c[f], 127, 1))
                    other = at(src, f, 1 - st, lt)
                    above = jnp.where(sub == 0, c[f] if st == 0 else pltpu.roll(other, 1, 0), pltpu.roll(c[f], 1, 0))
                    below = jnp.where(sub == 7, c[f] if st == 1 else pltpu.roll(other, 7, 0), pltpu.roll(c[f], 7, 0))
                    four[f] = 2.0 * (left[f] + right[f] + o[f]) + (above + below)
                e = 0.06 * c[1] + 0.1 * (four[0] + (left[2] - right[2]))
                n = 0.1 * (four[1] + sign * o[2]) - 0.06 * c[0]
                h = 0.1 * (four[2] + (left[0] - right[0]) + sign * o[1])
                put(st, lt, (e, n, h))

    def put_edge(st, lt, new):
        for f in range(3):
            edge[f * 16 + st * 8 : f * 16 + st * 8 + 8, lt * 128 : lt * 128 + 128] = new[f]

    full(near, far, put_edge)
    for lt in range(8):
        for st in range(2):
            y = upright([at(near, f, st, lt) for f in range(3)], sign)
            z = upright(y, sign)
            for f in range(3):
                rows, cols = slice(f * 16 + st * 8, f * 16 + st * 8 + 8), slice(lt * 128, lt * 128 + 128)
                mid[rows, cols] = y[f]
                kept[48 + f * 16 + st * 8 : 48 + f * 16 + st * 8 + 8, cols] += z[f]

    def put_kept(st, lt, new):
        for f in range(3):
            kept[f * 16 + st * 8 : f * 16 + st * 8 + 8, lt * 128 : lt * 128 + 128] += new[f]

    full(mid, edge, put_kept)


def column_terms(tiles, comp):
    lane, sub = lanes(), sublanes()
    flip = jnp.where(comp == 1, 1.0, -1.0)
    right_half = comp == 1
    x1, x2 = [[], [], []], [[], [], []]
    for v in tiles:
        w = pltpu.roll(v, 127, 1)
        a = jnp.where(right_half, w, v)
        b = jnp.where(right_half, v, w)
        for f in range(3):
            x1[f].append(pltpu.roll(a, (128 - 32 * f) % 128, 1))
            x2[f].append(pltpu.roll(b, (128 - 32 * f) % 128, 1))

    def lateral(v):
        per_tile = [sideways([v[f][k] for f in range(3)], flip) for k in range(len(v[0]))]
        return [[p[f] for p in per_tile] for f in range(3)]

    def full(c, out):
        res = [[], [], []]
        for rt in range(2):
            prev, nxt, four = {}, {}, {}
            for f in range(3):
                v = c[f][rt]
                p = c[f][2] if rt == 0 else c[f][0]
                q = c[f][1] if rt == 0 else c[f][2]
                prev[f] = jnp.where(sub == 0, pltpu.roll(p, 1, 0), pltpu.roll(v, 1, 0))
                nxt[f] = jnp.where(sub == 7, pltpu.roll(q, 7, 0), pltpu.roll(v, 7, 0))
                above = jnp.where(lane < 2, v, pltpu.roll(v, 2, 1))
                below = jnp.where(lane >= 30, v, pltpu.roll(v, 126, 1))
                four[f] = 2.0 * (prev[f] + nxt[f] + out[f][rt]) + (above + below)
            res[0].append(0.06 * c[1][rt] + 0.1 * (four[0] + flip * out[2][rt]))
            res[1].append(0.1 * (four[1] + (prev[2] - nxt[2])) - 0.06 * c[0][rt])
            res[2].append(0.1 * (four[2] + flip * out[0][rt] + (prev[1] - nxt[1])))
        return res

    y = lateral(x1)
    s0 = full(y, full(x1, x2))
    s1 = lateral([[v[0], v[1]] for v in y])
    pairs = []
    for f in range(3):
        row = []
        for rt in range(2):
            a = jnp.where(right_half, s0[f][rt], s1[f][rt])
            b = jnp.where(right_half, s1[f][rt], s0[f][rt])
            row.append(jnp.where(lane % 2 == 0, a, pltpu.roll(b, 1, 1)))
        pairs.append(row)
    return pairs


def rows_kernel(pay_up, pay_dn, x_own, rb, out_x, ke, halo_rows, mid, edge, kept, sems):
    comp = lax.axis_index("comp")
    loads = [
        [
            pltpu.make_async_copy(rb.at[pl.ds(k * 96, 96), :], kept.at[pl.ds(k * 96, 96), :], sems.at[2 * k]),
            pltpu.make_async_copy(pay.at[pl.ds(0, 96), :], halo_rows.at[k], sems.at[2 * k]),
        ]
        for k, pay in enumerate((pay_up, pay_dn))
    ]
    for c in loads[0] + loads[1]:
        c.start()
    rest = pl.multiple_of(comp * 128, 128)
    es = pl.multiple_of((1 - comp) * (COLS - 128), 128)
    puts = [
        pltpu.make_async_copy(
            kept.at[pl.ds((k * 3 + f) * 16, 16), pl.ds(rest, COLS - 128)],
            out_x.at[f, :, r, pl.ds(rest, COLS - 128)],
            sems.at[1],
        )
        for k, r in enumerate((0, 1, 15, 14))
        for f in range(3)
    ]
    for side, there in enumerate(neighbours()):
        for c in loads[side]:
            c.wait()

        @pl.when(there)
        def _():
            rows = halo_rows.at[side]
            row_terms(
                rows.at[pl.ds(0, 48)], rows.at[pl.ds(48, 48)], mid, edge,
                kept.at[pl.ds(side * 96, 96)], 1.0 if side == 0 else -1.0,
            )

        for c in puts[side * 6 : side * 6 + 6]:
            c.start()
    puts.append(pltpu.make_async_copy(kept.at[:, pl.ds(es, 128)], ke, sems.at[1]))
    puts[-1].start()
    for c in puts:
        c.wait()


def rows(pay_up, pay_dn, x_own, rb):
    sds = jax.ShapeDtypeStruct
    return pl.pallas_call(
        rows_kernel,
        out_shape=(sds(x_own.shape, F32), sds((192, 128), F32)),
        in_specs=[ANY] * 4,
        out_specs=(ANY, ANY),
        input_output_aliases={2: 0},
        scratch_shapes=[
            pltpu.VMEM((2, 96, COLS), F32),
            pltpu.VMEM((48, COLS), F32),
            pltpu.VMEM((48, COLS), F32),
            pltpu.VMEM((192, COLS), F32),
            pltpu.SemaphoreType.DMA((3,)),
        ],
        compiler_params=pltpu.CompilerParams(vmem_limit_bytes=VMEM_ALL),
        name="rows",
    )(pay_up, pay_dn, x_own, rb)


def final_kernel(
    x, ex, air, flow, warm, water, part, tally, wgt, pay_up, pay_dn, swp, x_own, ke, cb,
    out_x, out_flow, out_warm,
    s0, s1, kept, cbv, cbo, coef, blocks, wv, res, oc, mask, of, ow, small, sems,
):
    comp = lax.axis_index("comp")
    tile = lax.axis_index("tile")
    lane, sub = lanes(), sublanes()
    has_above, has_below = neighbours()

    def halo(pay, rows, third):
        out = []
        for d in range(2):
            for f in range(3):
                for lv in range(3 - d):
                    out.append((pay.at[(d * 3 + f) * 16 + lv, :], s0.at[f, lv, rows[d], pl.ds(0, COLS)]))
        for f in range(3):
            out.append((pay.at[104 + f, :], s0.at[f, 0, rows[2], pl.ds(0, COLS)]))
        to = pl.ds(0, OCOLS)
        for k in range(2):
            out.append((pay.at[107 + k, :], coef.at[k, rows[0], :]))
            cols = pl.ds(k * OCOLS, OCOLS)
            out.append((pay.at[pl.ds(96, 8), cols], oc.at[pl.ds(k * 10, 8), third, to]))
            for lv in (8, 9):
                out.append((pay.at[101 + lv, cols], oc.at[k * 10 + lv, third, to]))
        out.append((pay.at[111, to], oc.at[20, third, to]))
        return [pltpu.make_async_copy(a, b, sems.at[1]) for a, b in out]

    above = ((23, 22, 21), 8)
    below = ((16, 17, 18), 15)
    keeps = [pltpu.make_async_copy(ke, kept, sems.at[2]), pltpu.make_async_copy(cb, cbv, sems.at[2])]
    smalls = [pltpu.make_async_copy(swp, small, sems.at[3])]
    mine = [
        pltpu.make_async_copy(x.at[:, pl.ds(0, 3)], s0.at[:, :, pl.ds(0, 16), pl.ds(0, COLS)], sems.at[4]),
        pltpu.make_async_copy(ex, coef.at[0, pl.ds(0, 16), :], sems.at[4]),
        pltpu.make_async_copy(air, coef.at[1, pl.ds(0, 16), :], sems.at[4]),
        pltpu.make_async_copy(flow.at[0], oc.at[pl.ds(0, 10), pl.ds(0, 8), pl.ds(0, OCOLS)], sems.at[4]),
        pltpu.make_async_copy(flow.at[1], oc.at[pl.ds(10, 10), pl.ds(0, 8), pl.ds(0, OCOLS)], sems.at[4]),
        pltpu.make_async_copy(warm, oc.at[20, pl.ds(0, 8), pl.ds(0, OCOLS)], sems.at[4]),
        pltpu.make_async_copy(water, mask, sems.at[4]),
    ]
    wcopy = pltpu.make_async_copy(wgt, wv, sems.at[5])

    halos = halo(pay_up, *above) + halo(pay_dn, *below)
    for c in smalls + mine + halos + keeps + [wcopy]:
        c.start()
    for c in smalls:
        c.wait()

    row_ok = jnp.where(sub >= 4, has_above.astype(jnp.int32), has_below.astype(jnp.int32)) > 0
    row_halo = jnp.where(sub < 4, has_above.astype(jnp.int32), has_below.astype(jnp.int32)) > 0
    edge2 = jnp.where(comp == 0, lane, 127 - lane) < 2
    edge1 = jnp.where(comp == 0, lane, 127 - lane) < 1
    corner = jnp.where(row_ok, small[24:32, :], 0.0)
    for f in range(3):
        for lv in range(3):
            shift = (128 - 2 * (f * 16 + lv) + 126 * comp) % 128
            for rt in range(3):
                v = small[rt * 8 : rt * 8 + 8, :] if rt < 2 else corner
                s0[f, lv, rt * 8 : rt * 8 + 8, COLS:WIDE] = jnp.where(edge2, pltpu.roll(v, shift, 1), 0.0)

    for c in mine:
        c.wait()
    for c in halos:
        c.wait()

    @pl.when(jnp.logical_not(has_above & has_below))
    def _():
        for lt in range(8):
            cols = slice(lt * 128, lt * 128 + 128)
            for f in range(3):
                for lv in range(3):
                    s0[f, lv, 16:24, cols] = jnp.where(row_ok, s0[f, lv, 16:24, cols], 0.0)

        def oclear(g, _):
            for lt in range(4):
                cols = slice(lt * 128, lt * 128 + 128)
                oc[g, 8:16, cols] = jnp.where(row_halo, oc[g, 8:16, cols], 0.0)
            return 0

        lax.fori_loop(0, 21, oclear, 0)

    for level in range(2):

        def put_first(rt, lt, new):
            rows, cols = slice(rt * 8, rt * 8 + 8), slice(lt * 128, lt * 128 + 128)
            for f in range(3):
                v = new[f]
                if lt == 8:
                    v = jnp.where(edge1 & row_ok if rt == 2 else edge1, v, 0.0)
                elif rt == 2:
                    v = jnp.where(row_ok, v, 0.0)
                s1[f, level, rows, cols] = v

        sweep(s0, level, 0, level + 1, range(3), range(9), True, None, put_first)

    def put_flux(rt, lt, new):
        rows, cols = slice(rt * 8, rt * 8 + 8), slice(lt * 128, lt * 128 + 128)
        e, n, h = new
        mult = coef[0, rows, cols] * jnp.sqrt(e * e + n * n + 0.25)
        at = rt * 512 + lt * 8
        for f, v in enumerate((mult * e, mult * n, mult * (coef[1, rows, cols] - h))):
            hi = v.astype(jnp.bfloat16).astype(F32)
            blocks[pl.ds(at + f, 8, stride=64), :] = hi
            blocks[pl.ds(at + 3 + f, 8, stride=64), :] = v - hi
        blocks[pl.ds(at + 6, 8, stride=64), :] = jnp.ones((8, 128), F32)
        blocks[pl.ds(at + 7, 8, stride=64), :] = jnp.zeros((8, 128), F32)

    sweep(s1, 0, 0, 1, range(3), range(8), True, None, put_flux)

    for c in keeps:
        c.wait()
    es = pl.multiple_of((1 - comp) * (COLS - 128), 128)
    pairs = column_terms((small[0:8, :], small[8:16, :], corner), comp)
    own2 = jnp.where(comp == 0, 127 - lane, lane) < 2
    for f in range(3):
        for lv in range(16):
            shift = (128 - 2 * lv + 126 * (1 - comp)) % 128
            for rt in range(2):
                v = cbv[f, lv, rt * 8 : rt * 8 + 8, :]
                for k, at in ((0, 0), (1, 1)) if rt == 0 else ((2, 7), (3, 6)):
                    line = kept[(k * 3 + f) * 16 + lv : (k * 3 + f) * 16 + lv + 1, :]
                    v = jnp.where(sub == at, line, v)
                v = v + jnp.where(own2, pltpu.roll(pairs[f][rt], shift, 1), 0.0)
                cbo[f, lv, rt * 8 : rt * 8 + 8, :] = v
    put_edge = pltpu.make_async_copy(cbo, out_x.at[:, :, :, pl.ds(es, 128)], sems.at[7])
    put_edge.start()

    wcopy.wait()
    base = tile * 128

    def remap(g, _):
        live = tally[g]
        parts = []
        for s in range(4):
            p = part[s, g] - base
            p = jnp.where(p < 0, p + 192, p)
            row = pl.multiple_of(p * 8, 8)
            v = blocks[pl.ds(row, 8), :]
            parts.append(v * jnp.where(s < live, 1.0, 0.0))
        lhs = jnp.concatenate(parts, axis=1).astype(jnp.bfloat16)
        rhs = wv[g].reshape(512, 128)
        res[pl.ds(pl.multiple_of(g * 8, 8), 8), :] = jnp.dot(lhs, rhs, preferred_element_type=F32)
        return 0

    lax.fori_loop(0, 32, remap, 0, unroll=32)

    def unpack_ocean():
        for g in range(21):
            shift = (128 - g + 127 * comp) % 128
            v = pltpu.roll(small[16:24, :], shift, 1)
            oc[g, 0:8, OCOLS:OWIDE] = jnp.where(edge1, v, 0.0)

    unpack_ocean()

    def around(g, lt):
        cols = slice(lt * 128, lt * 128 + 128)
        c = oc[g, 0:8, cols]
        hv = oc[g, 8:16, cols]
        lo, hi = (lt - 1) % 5, lt + 1
        left = jnp.where(lane == 0, pltpu.roll(oc[g, 0:8, lo * 128 : lo * 128 + 128], 1, 1), pltpu.roll(c, 1, 1))
        right = jnp.where(lane == 127, pltpu.roll(oc[g, 0:8, hi * 128 : hi * 128 + 128], 127, 1), pltpu.roll(c, 127, 1))
        prev = jnp.where(sub == 0, hv, pltpu.roll(c, 1, 0))
        nxt = jnp.where(sub == 7, hv, pltpu.roll(c, 7, 0))
        return c, left, right, prev, nxt

    for lt in range(4):
        cols = slice(lt * 128, lt * 128 + 128)
        m = mask[:, cols].astype(F32)
        den = res[pl.ds(lt * 8 + 6, 8, stride=32), :]
        rem = [
            (res[pl.ds(lt * 8 + f, 8, stride=32), :] + res[pl.ds(lt * 8 + f + 3, 8, stride=32), :]) / den
            for f in range(3)
        ]
        for k in range(2):
            for lv in range(10):
                g = k * 10 + lv
                c, left, right, prev, nxt = around(g, lt)
                other = oc[(1 - k) * 10 + lv, 0:8, cols]
                vert = oc[k * 10 + max(lv - 1, 0), 0:8, cols] + oc[k * 10 + min(lv + 1, 9), 0:8, cols]
                v = 0.2 * ((left + right) + (prev + nxt)) + 0.1 * vert
                v = v + (0.06 if k == 0 else -0.06) * other
                if lv == 0:
                    v = v + 0.2 * rem[k]
                of[k, lv, :, cols] = m * v
        c, left, right, prev, nxt = around(20, lt)
        lap = (left + right) + (prev + nxt) - 4.0 * c
        carried = oc[0, 0:8, cols] * (0.5 * (right - left)) + oc[10, 0:8, cols] * (0.5 * (nxt - prev))
        ow[:, cols] = c + (m * 0.2) * (rem[2] - carried + 0.5 * lap)
    tail = [
        pltpu.make_async_copy(of, out_flow, sems.at[8]),
        pltpu.make_async_copy(ow, out_warm, sems.at[8]),
    ]
    for c in tail:
        c.start()
    for c in tail + [put_edge]:
        c.wait()


def final(x, ex, air, flow, warm, water, part, tally, wgt, halos, kept):
    sds = jax.ShapeDtypeStruct
    return pl.pallas_call(
        final_kernel,
        out_shape=(sds(x.shape, F32), sds(flow.shape, F32), sds(warm.shape, F32)),
        in_specs=[ANY] * 6 + [SMEM] * 2 + [ANY] * 7,
        out_specs=(ANY, ANY, ANY),
        input_output_aliases={12: 0},
        scratch_shapes=[
            pltpu.VMEM((3, 3, 24, WIDE), F32),
            pltpu.VMEM((3, 2, 24, WIDE), F32),
            pltpu.VMEM((192, 128), F32),
            pltpu.VMEM((3, LEV, ROWS, 128), F32),
            pltpu.VMEM((3, LEV, ROWS, 128), F32),
            pltpu.VMEM((2, 24, COLS), F32),
            pltpu.VMEM((24 * 64, 128), F32),
            pltpu.VMEM((32, 4, 128, 128), jnp.bfloat16),
            pltpu.VMEM((256, 128), F32),
            pltpu.VMEM((21, 16, OWIDE), F32),
            pltpu.VMEM((OROWS, OCOLS), jnp.int32),
            pltpu.VMEM((2, OLEV, OROWS, OCOLS), F32),
            pltpu.VMEM((OROWS, OCOLS), F32),
            pltpu.VMEM((32, 128), F32),
            pltpu.SemaphoreType.DMA((9,)),
        ],
        compiler_params=pltpu.CompilerParams(vmem_limit_bytes=VMEM_ALL),
        name="final",
    )(x, ex, air, flow, warm, water, part, tally, wgt, *halos, *kept)


def shift(v, step, across):
    tiles = lax.axis_size("tile")
    if not across:
        return lax.ppermute(v, "tile", [(t, (t + step) % tiles) for t in range(tiles)])
    perm = [(c * tiles + t, (1 - c) * tiles + (t + step) % tiles) for c in range(2) for t in range(tiles)]
    return lax.ppermute(v, ("comp", "tile"), perm)


def shards(x, ex, air, flow, warm, water, part, tally, wgt):
    pay_up, pay_dn, swp = pack(x, ex, air, flow, warm)
    got_up = shift(pay_up, 1, False)
    pay_dn, *kept = own(x, True, [pay_dn])
    got_dn = shift(pay_dn, -1, False)
    swp, x_own, rb, cb = own(x, False, [swp, *kept])
    upper = lax.broadcasted_iota(jnp.int32, (8, 128), 0) >= 4
    corner = jnp.where(upper, got_up[112:120, :128], got_dn[112:120, :128])
    got_sw = shift(lax.dynamic_update_slice(swp, corner, (24, 0)), 0, True)
    x_own, ke = rows(got_up, got_dn, x_own, rb)
    return final(x, ex, air, flow, warm, water, part.T, tally, wgt, (got_up, got_dn, got_sw), (x_own, ke, cb))


def solution(mesh):
    placed = (
        P(None, None, "tile", "comp"),
        P("tile", "comp"),
        P("tile", "comp"),
        P(None, None, "tile", "comp"),
        P("tile", "comp"),
        P("tile", "comp"),
        P(("comp", "tile"), None),
        P(("comp", "tile")),
        P(("comp", "tile"), None, None, None),
    )
    return jax.shard_map(
        shards,
        mesh=mesh,
        in_specs=placed,
        out_specs=(P(None, None, "tile", "comp"), P(None, None, "tile", "comp"), P("tile", "comp")),
        check_vma=False,
    )
```
